32 devices in a mesh: frame: 16 (over z, y, x), head: 2 (over core).
Axes of the slice: x: 2, y: 2, z: 4, core: 2. Of those that a mesh axis runs over, the one named last changes fastest.
Arguments:
- residual: bfloat16 [2048, 5120], P('frame', 'head'), may hold values from -48 to 48
- query_proj: bfloat16 [2048, 3072], P('frame', 'head'), may hold values from -200 to 200
- key_proj: bfloat16 [2048, 3072], P('frame', 'head'), may hold values from -200 to 200
- value_proj: bfloat16 [2048, 3072], P('frame', 'head'), may hold values from -6 to 6
- q_gain: float32 [3072], P('head'), may hold values from 1 to 3
- k_gain: float32 [3072], P('head'), may hold values from 1 to 3
- time_embed: float32 [5120], P(('frame', 'head')), may hold values from -6 to 6
- time_proj: bfloat16 [5120, 3, 5120], P(('frame', 'head')), may hold values from -0.15625 to 0.15625
- mod_table: float32 [3, 5120], P(None, 'head'), may hold values from -3 to 3
- out_weight: bfloat16 [3072, 5120], P('head'), may hold values from -0.109375 to 0.109375
Outputs:
- hidden_out: bfloat16 [2048, 5120], P('frame', 'head')
- mlp_input: bfloat16 [2048, 5120], P('frame', 'head')
The draws below stay inside these ranges and needn't reach their ends.
All inputs are finite; a program needn't handle non-finite values.
Results may differ from the reference program's by a relative error of at most 0.0071.
Values may be sent and summed in bfloat16 or wider, within the bound.
A program may use at most 128 MiB of HBM per device.

```python
import math
import jax
import jax.numpy as jnp
from jax import lax

D = 5120
HEADS = 24
HD = 128
TOK_DEV = 128
HQ = 3072
TOKENS = 2048


def draw_residual(key, part):
    key_base, key_rows, key_cols = jax.random.split(key, 3)
    base = jnp.clip(jax.random.normal(key_base, (TOKENS, D)), -4.0, 4.0)
    rows = jnp.exp(jax.random.uniform(key_rows, (TOKENS, 1), minval=math.log(0.25), maxval=math.log(2.5)))
    trend = math.log(3.0) * jnp.arange(D, dtype=jnp.float32) / D
    cols = jnp.exp(trend + jax.random.uniform(key_cols, (D,), minval=-0.35, maxval=0.35))
    return (base * rows * cols).astype(jnp.bfloat16)


def random_field(key_base, key_rows, key_cols):
    base = jnp.clip(jax.random.normal(key_base, (TOKENS, HQ)), -4.0, 4.0)
    rows = jnp.exp(jax.random.uniform(key_rows, (TOKENS, 1), minval=0.0, maxval=math.log(10.0)))
    trend = 0.5 * math.log(3.0) * jnp.arange(HQ, dtype=jnp.float32) / HQ
    cols = jnp.exp(trend + jax.random.uniform(key_cols, (HQ,), minval=-1.0, maxval=1.0))
    return base * rows * cols


def paired_fields(key):
    seeds = jax.random.split(key, 6)
    queries = random_field(seeds[0], seeds[1], seeds[2])
    keys_field = random_field(seeds[3], seeds[4], seeds[5])
    return (queries, keys_field)


def draw_query_proj(key, part):
    return paired_fields(key)[0].astype(jnp.bfloat16)


def draw_key_proj(key, part):
    return paired_fields(key)[1].astype(jnp.bfloat16)


def strengthened(entries, rng, source, target, shards_of, factor):
    owner, partner = [(jnp.arange(entries.shape[position]) // (entries.shape[position] // shards_of)).reshape([-1 if axis == position else 1 for axis in range(entries.ndim)]) for position in (source, target)]
    chosen = jax.random.permutation(rng, shards_of)[partner]
    strong = (owner == chosen) | (owner == (partner + shards_of // 2) % shards_of)
    return jnp.where(strong, factor * entries, entries)


def steps_of(rng, shape, cuts, least, largest):
    def one(dim, blocks):
        draws = jax.random.uniform(jax.random.fold_in(jax.random.fold_in(rng, 6), dim), (blocks,), jnp.float32, least / len(cuts), largest / len(cuts))
        return jnp.repeat(jnp.exp(draws), shape[dim] // blocks).reshape((-1,) + (1,) * (len(shape) - dim - 1))

    loudness = one(*cuts[0])
    for cut in cuts[1:]:
        loudness = loudness * one(*cut)
    return loudness


def scatter_about(stream_key, dims, scale, reach, cuts=(), kind=jnp.bfloat16):
    array = jax.random.normal(stream_key, dims, jnp.float32) * scale
    if len(cuts) > 0:
        array = steps_of(stream_key, dims, cuts, -0.22, 0.18) * array
    return jnp.clip(array, min=-reach, max=reach).astype(kind)


def gaussian_with(stream_key, extent, deviation, reach, shards, heavy, held_as=jnp.bfloat16):
    entries = deviation * jax.random.normal(stream_key, extent, jnp.float32)
    if shards:
        entries = entries * steps_of(stream_key, extent, shards, -0.22, 0.18)
    return jnp.clip(strengthened(entries, jax.random.fold_in(stream_key, 3), *heavy), -reach, reach).astype(held_as)


def setup_inputs(seed: int = 0) -> dict:
    keys = jax.random.split(jax.random.key(seed), 11)
    return {
        "residual": draw_residual(jax.random.fold_in(keys[10], 71), 0),
        "query_proj": draw_query_proj(jax.random.fold_in(keys[10], 71), 0),
        "key_proj": draw_key_proj(jax.random.fold_in(keys[10], 71), 0),
        "value_proj": scatter_about(keys[3], (TOKENS, HQ), 1.0, 6.0, ((0, 16), (1, 2))),
        "q_gain": jnp.clip(jnp.exp(math.log(3.0) - 1.0986123 * jax.random.uniform(keys[4], (HQ,), jnp.float32) ** steps_of(keys[4], (HQ,), ((0, 2),), -0.2, 0.2)), 1.0, 3.0),
        "k_gain": jnp.clip(jnp.exp(math.log(3.0) - 1.0986123 * jax.random.uniform(keys[5], (HQ,), jnp.float32) ** steps_of(keys[5], (HQ,), ((0, 2),), -0.2, 0.2)), 1.0, 3.0),
        "time_embed": scatter_about(keys[6], (D,), 1.5, 6.0, ((0, 32),), jnp.float32),
        "time_proj": gaussian_with(keys[7], (D, 3, D), D ** -0.5, 0.15625, ((0, 32),), (0, 2, 32, 2.75)),
        "mod_table": scatter_about(keys[8], (3, D), 0.5, 3.0, ((1, 2),), jnp.float32),
        "out_weight": scatter_about(keys[9], (HQ, D), HQ ** -0.5, 0.109375, ((0, 2),)),
    }


def reference(residual, query_proj, key_proj, value_proj, q_gain, k_gain, time_embed, time_proj, mod_table, out_weight):
    emb = jax.nn.silu(time_embed)
    modulation = mod_table + jnp.einsum('r,rcd->cd', emb, time_proj.astype(jnp.float32), precision=lax.Precision.HIGHEST)
    gate = modulation[0]
    shift = modulation[1]
    scale = modulation[2]
    query_wide = query_proj.astype(jnp.float32)
    key_wide = key_proj.astype(jnp.float32)
    query_rms = lax.rsqrt(lax.optimization_barrier(jnp.sum(query_wide * query_wide, axis=1)) / (HEADS * HD) + 1e-06)
    key_rms = lax.rsqrt(lax.optimization_barrier(jnp.sum(key_wide * key_wide, axis=1)) / (HEADS * HD) + 1e-06)
    query_normed = (query_wide * query_rms[:, None] * q_gain).astype(jnp.bfloat16)
    key_normed = (key_wide * key_rms[:, None] * k_gain).astype(jnp.bfloat16)
    inv_root = 1.0 / math.sqrt(HD)
    q_heads = query_normed.reshape(TOKENS, HEADS, HD).transpose(1, 0, 2)
    k_heads = key_normed.reshape(TOKENS, HEADS, HD).transpose(1, 0, 2)
    v_heads = value_proj.reshape(TOKENS, HEADS, HD).transpose(1, 0, 2)

    def head_attend(packed):
        q_head, k_head, v_head = packed
        values = v_head.astype(jnp.float32)

        def block(q_block):
            scores = jnp.dot(q_block, k_head.T, preferred_element_type=jnp.float32) * inv_root
            top = lax.optimization_barrier(jnp.max(scores, axis=1, keepdims=True))
            weights = jnp.exp(scores - top)
            total = lax.optimization_barrier(jnp.sum(weights, axis=1, keepdims=True))
            return jnp.dot(weights, values, precision=lax.Precision.HIGHEST) / total
        blocks = lax.map(block, q_head.reshape(TOKENS // TOK_DEV, TOK_DEV, HD))
        return blocks.reshape(TOKENS, HD)
    attn_heads = lax.map(head_attend, (q_heads, k_heads, v_heads))
    attn = attn_heads.transpose(1, 0, 2).reshape(TOKENS, HEADS * HD).astype(jnp.bfloat16)
    proj = jnp.dot(attn, out_weight, preferred_element_type=jnp.float32)
    hidden_out = (residual.astype(jnp.float32) + gate * proj).astype(jnp.bfloat16)
    hidden32 = lax.optimization_barrier(hidden_out).astype(jnp.float32)
    mean = lax.optimization_barrier(jnp.sum(hidden32, axis=1, keepdims=True)) / D
    var = lax.optimization_barrier(jnp.sum(hidden32 * hidden32, axis=1, keepdims=True)) / D - mean * mean
    mlp_input = ((hidden32 - mean) * lax.rsqrt(var + 1e-06) * (1.0 + scale) + shift).astype(jnp.bfloat16)
    return (hidden_out, mlp_input)
```

```python
import math

import jax
import jax.numpy as jnp
from jax import lax
from jax.experimental import pallas as pl
from jax.experimental.pallas import tpu as pltpu
from jax.sharding import PartitionSpec as P

D = 5120
HEADS = 24
HD = 128


MESH = pl.DeviceIdType.MESH
PLANE = 4
LINE = 4
TILE = 512
FAR = (1, 3, 2)
KEY, VALUE, QUERY = 0, 1, 2
BEAT = 2.9
LAG = 4.0


def remote(src, dst, send, recv, device):
    return pltpu.make_async_remote_copy(
        src_ref=src, dst_ref=dst, send_sem=send, recv_sem=recv, device_id=device, device_id_type=MESH
    )


WINDOW = 3
AHEAD = 3


def agenda(heads):
    queue = [(b, h) for h in range(heads) for b in (VALUE, KEY, QUERY)]
    steps = [(4.0, ("mod", 0)), (7.0, ("mod", 1)), (11.0, ("mod", 2))]
    arrive = {}
    for beat, (b, h) in enumerate(queue):
        for n, d in enumerate(FAR):
            arrive[b, h, d] = BEAT * beat + 2.0 + 0.8 * n
        opened = BEAT * (beat - WINDOW) + 2.0 + 0.8 * 2 + 0.01 if beat >= AHEAD else 0.0
        arrive[b, h, 0] = opened
        if beat >= AHEAD:
            steps.append((opened, ("launch", b, h)))
    for h in range(heads):
        for d in (0,) + FAR:
            for b in (VALUE, KEY):
                at = arrive[b, h, d]
                if d:
                    steps.append((at, ("first", d, h, b)))
                steps.append((at + LAG, ("second", d, h, b)))
                steps.append((at + 2 * LAG, ("third", d, h, b)))
        for d in FAR:
            steps.append((arrive[QUERY, h, d], ("query", d, h)))
        ready = max(arrive[QUERY, h, d] for d in FAR)
        for d in (0,) + FAR:
            ready = max(ready, max(arrive[b, h, d] + 2 * LAG for b in (VALUE, KEY))) + 0.01
            steps.append((ready, ("absorb", d, h)))
    return [step for _, step in sorted(steps, key=lambda pair: pair[0])]


def block_kernel(
    q_hbm, k_hbm, v_hbm, qg_ref, kg_ref, te_ref, table_ref, res_hbm, proj_hbm, weight_hbm,
    hidden_ref, row_ref, mod_ref,
    qraw, kraw, qn, kn, kbuf, vbuf, qbuf, obuf, arecv, top, total, summed,
    squares, squares_in, rms, part, mpart, macc, mrs, mz, mfin, tbuf, wbuf, rbuf, pacc, pout, pin, stat, stat_in,
    own_sem, load_sem, zs, zr, xs, xr, ys, yr, dxs, dxr, dys, dyr, os, orr, ms, mr, ps, pr, ss, sr,
):
    f32, bf = jnp.float32, jnp.bfloat16
    frames = LINE * PLANE
    f = lax.axis_index("frame")
    hd = lax.axis_index("head")
    z = lax.div(f, PLANE)
    x = lax.rem(f, 2)
    y = lax.rem(lax.div(f, 2), 2)
    step_x = 1 - 2 * x
    step_y = 2 - 4 * y
    to_x = {"frame": f + step_x}
    to_y = {"frame": f + step_y}
    to_xy = {"frame": f + step_x + step_y}
    to_pair = {"head": 1 - hd}
    rows, cols_all = qn.shape
    half = rows // 2
    width = cols_all // LINE
    heads = width // HD
    owned = hidden_ref.shape[1]
    quarter = owned // PLANE

    def later(d):
        return lax.rem(f + PLANE * d, frames)

    def earlier(d):
        return lax.rem(f + frames - PLANE * d, frames)

    def piece(ref, line, h):
        return ref.at[:, pl.ds(pl.multiple_of(line * width + h * HD, HD), HD)]

    def quarter_of(ref, spot):
        return ref.at[:, pl.ds(pl.multiple_of(spot * quarter, 128), quarter)]

    sends = []

    def send(src, dst, s, r, peer):
        copy = remote(src, dst, s, r, peer)
        copy.start()
        sends.append(copy)

    barrier = pltpu.get_barrier_semaphore()
    for d in range(1, LINE):
        pl.semaphore_signal(barrier, inc=1, device_id={"frame": later(d)}, device_id_type=MESH)
    for peer in (to_x, to_y, to_xy, to_pair):
        pl.semaphore_signal(barrier, inc=1, device_id=peer, device_id_type=MESH)

    raw = []
    for i, (src, dst) in enumerate(((q_hbm, qraw), (k_hbm, kraw))):
        raw.append(pltpu.make_async_copy(src, dst, load_sem.at[i]))
        raw[i].start()
    loads = [pltpu.make_async_copy(proj_hbm, tbuf, load_sem.at[2])]
    loads.append(pltpu.make_async_copy(res_hbm, rbuf, load_sem.at[3]))
    for h in range(heads):
        for j in range(LINE):
            at = pl.ds(j * width + h * HD, HD)
            loads.append(
                pltpu.make_async_copy(weight_hbm.at[at], wbuf.at[h, pl.ds(j * HD, HD)], load_sem.at[4 + h * LINE + j])
            )
    for i, ref in enumerate((qraw, kraw)):
        raw[i].wait()
        lanes = jnp.zeros((rows, 128), f32)
        for c in range(0, cols_all, 128):
            wide = ref[:, c : c + 128].astype(f32)
            lanes += wide * wide
        squares[i] = lanes
    pl.semaphore_wait(barrier, LINE + 3)

    bufs = (kbuf, vbuf)
    own = {}

    def number(h, d, b):
        return (h * LINE + d) * 2 + b

    def send_line(b, h, src, dst):
        for d in FAR:
            peer = later(d)
            n = (b * heads + h) * 3 + d - 1
            send(piece(src, lax.div(peer, PLANE), h), dst, zs.at[n], zr.at[n], {"frame": peer})

    def send_own(b, h, src, dst):
        mine = piece(src, z, h)
        if b != QUERY:
            n = number(h, 0, b)
            send(mine, dst, xs.at[n], xr.at[n], to_x)
            send(mine, dst, ys.at[n], yr.at[n], to_y)
        own[b, h] = pltpu.make_async_copy(mine, dst, own_sem.at[b * heads + h])
        own[b, h].start()

    def launch(b, h):
        if b == VALUE:
            src, dst = v_hbm, vbuf.at[h, f]
        else:
            i, ref, gain, src, dst = (
                (1, kraw, kg_ref, kn, kbuf.at[h, f]) if b == KEY else (0, qraw, qg_ref, qn, qbuf.at[h, z])
            )
            for j in range(LINE):
                at = slice(j * width + h * HD, j * width + (h + 1) * HD)
                src[:, at] = (ref[:, at].astype(f32) * rms[i, :, 0:1] * gain[at].reshape(1, HD)).astype(bf)
        send_line(b, h, src, dst)
        send_own(b, h, src, dst)

    send(squares, squares_in, ss.at[0], sr.at[0], to_pair)
    launch(VALUE, 0)
    for copy in loads:
        copy.start()

    remote(squares, squares_in, ss.at[0], sr.at[0], to_pair).wait_recv()
    for i in range(2):
        sums = jnp.sum(squares[i] + squares_in[i], axis=1, keepdims=True)
        rms[i] = jnp.broadcast_to(lax.rsqrt(sums / (HEADS * HD) + 1e-06), (rows, 128))
    for b, h in [(b, h) for h in range(heads) for b in (VALUE, KEY, QUERY)][1:AHEAD]:
        launch(b, h)

    def first(d, h, b):
        n = number(h, d, b)
        m = (b * heads + h) * 3 + d - 1
        at = earlier(d)
        block = bufs[b].at[h, at]
        remote(block, block, zs.at[m], zr.at[m], {"frame": at}).wait_recv()
        send(block, block, xs.at[n], xr.at[n], to_x)
        send(block, block, ys.at[n], yr.at[n], to_y)

    def second(d, h, b):
        n = number(h, d, b)
        at = earlier(d)
        block = bufs[b].at[h, at + step_x]
        remote(block, block, xs.at[n], xr.at[n], to_x).wait_recv()
        low = block.at[pl.ds(half, half)]
        send(low, low, dys.at[n], dyr.at[n], to_y)
        block = bufs[b].at[h, at + step_y]
        remote(block, block, ys.at[n], yr.at[n], to_y).wait_recv()
        high = block.at[pl.ds(0, half)]
        send(high, high, dxs.at[n], dxr.at[n], to_x)

    def third(d, h, b):
        n = number(h, d, b)
        block = bufs[b].at[h, earlier(d) + step_x + step_y]
        high = block.at[pl.ds(0, half)]
        remote(high, high, dxs.at[n], dxr.at[n], to_x).wait_recv()
        low = block.at[pl.ds(half, half)]
        remote(low, low, dys.at[n], dyr.at[n], to_y).wait_recv()

    def query(d, h):
        m = (QUERY * heads + h) * 3 + d - 1
        block = qbuf.at[h, lax.div(earlier(d), PLANE)]
        remote(block, block, zs.at[m], zr.at[m], {"frame": earlier(d)}).wait_recv()

    def absorb(d, h):
        opening, closing = d == 0, d == FAR[-1]
        if opening:
            for b in (KEY, VALUE, QUERY):
                own[b, h].wait()
        base = pl.multiple_of(lax.div(earlier(d), PLANE) * PLANE, PLANE)
        group = pl.ds(base, PLANE)

        def block_of(i, carry):
            keys = kbuf[h, group].reshape(PLANE * rows, HD)
            values = vbuf[h, group].reshape(PLANE * rows, HD)
            scores = lax.dot_general(
                qbuf[h, i], keys, (((1,), (1,)), ((), ())), preferred_element_type=f32
            ) * (1.0 / math.sqrt(HD))
            peak = jnp.max(scores, axis=1, keepdims=True)
            if not opening:
                old = top[h, i]
                peak = jnp.maximum(old, peak)
                fade = jnp.exp(old - peak)
            weights = jnp.exp(scores - peak)
            count = jnp.sum(weights, axis=1, keepdims=True)
            mixed = jnp.dot(weights.astype(bf), values, preferred_element_type=f32)
            if not opening:
                count = count + fade * total[h, i]
                mixed = mixed + fade * summed[h, i]
            if closing:
                obuf[h, i] = (mixed / count).astype(bf)
            else:
                top[h, i] = peak
                total[h, i] = count
                summed[h, i] = mixed
            return carry

        lax.fori_loop(0, LINE, block_of, 0, unroll=True)
        if closing:
            for e in FAR:
                n = h * 3 + e - 1
                send(
                    obuf.at[h, lax.div(later(e), PLANE)], arecv.at[h, z],
                    os.at[n], orr.at[n], {"frame": later(e)},
                )
            arecv[h, z] = obuf[h, z]

    spot = lax.rem(f, PLANE)
    plane = ((to_x, spot + step_x), (to_y, spot + step_y), (to_xy, spot + step_x + step_y))

    def mod(stage):
        if stage == 0:
            loads[0].wait()
            t = te_ref[...]
            emb = t / (1.0 + jnp.exp(-t))
            high = emb.astype(bf).astype(f32)
            middle = (emb - high).astype(bf).astype(f32)
            low = emb - high - middle
            row = lax.broadcasted_iota(jnp.int32, (8, emb.shape[1]), 0)
            split = jnp.where(row == 0, high, jnp.where(row == 1, middle, jnp.where(row == 2, low, 0.0)))
            split = split.astype(bf)
            for c in range(3):
                for side in range(2):
                    term = jnp.dot(
                        split, tbuf[c, :, side * owned : (side + 1) * owned], preferred_element_type=f32
                    )
                    part[side, c : c + 1, :] = jnp.sum(term, axis=0, keepdims=True)
            send(part.at[1 - hd], mpart, ms.at[0], mr.at[0], to_pair)
        elif stage == 1:
            remote(part.at[1 - hd], mpart, ms.at[0], mr.at[0], to_pair).wait_recv()
            macc[...] = part[hd] + mpart[...]
            for i, (peer, theirs) in enumerate(plane):
                send(quarter_of(macc, theirs), mrs.at[i + 1], ms.at[1 + i], mr.at[1 + i], peer)
            keep = pltpu.make_async_copy(quarter_of(macc, spot), mrs.at[0], own_sem.at[3 * heads])
            keep.start()
            keep.wait()
        elif stage == 2:
            for i, (peer, theirs) in enumerate(plane):
                remote(mrs.at[i + 1], mrs.at[i + 1], ms.at[1 + i], mr.at[1 + i], peer).wait_recv()
            mz[0] = (mrs[0] + mrs[1]) + (mrs[2] + mrs[3])
            for d in range(1, LINE):
                send(mz.at[0], mz.at[d], ms.at[3 + d], mr.at[3 + d], {"frame": later(d)})
        elif stage == 3:
            for d in range(1, LINE):
                remote(mz.at[0], mz.at[d], ms.at[3 + d], mr.at[3 + d], {"frame": earlier(d)}).wait_recv()
            mz[LINE] = (mz[0] + mz[2]) + (mz[1] + mz[3])
            mine = quarter_of(mfin, spot)
            for i, (peer, theirs) in enumerate(plane):
                send(mz.at[LINE], mine, ms.at[7 + i], mr.at[7 + i], peer)
            keep = pltpu.make_async_copy(mz.at[LINE], mine, own_sem.at[3 * heads])
            keep.start()
            keep.wait()
        else:
            for i, (peer, theirs) in enumerate(plane):
                block = quarter_of(mfin, theirs)
                remote(block, block, ms.at[7 + i], mr.at[7 + i], peer).wait_recv()
            mfin[...] = mfin[...] + table_ref[...]

    todo = {"launch": launch, "query": query, "first": first, "second": second, "third": third, "absorb": absorb, "mod": mod}
    for name, *of in agenda(heads):
        todo[name](*of)

    def gathered(h):
        for d in range(1, LINE):
            n = h * 3 + d - 1
            block = arecv.at[h, lax.div(earlier(d), PLANE)]
            remote(block, block, os.at[n], orr.at[n], {"frame": earlier(d)}).wait_recv()
        for copy in loads[2 + h * LINE : 2 + (h + 1) * LINE]:
            copy.wait()
        return jnp.concatenate([arecv[h, j] for j in range(LINE)], axis=1)

    def project(attn, h, side, at):
        begin = pl.multiple_of(side * owned + at, 128)
        return jnp.dot(attn, wbuf[h, :, pl.ds(begin, TILE)], preferred_element_type=f32)

    for h in range(heads - 1):
        attn = gathered(h)
        for side in range(2):
            for i in range(owned // TILE):
                at = slice(i * TILE, (i + 1) * TILE)
                share = project(attn, h, side, i * TILE)
                pacc[side, :, at] = share if h == 0 else pacc[side, :, at] + share
        if h == 0:
            mod(3)
    mod(4)
    loads[1].wait()
    attn = gathered(heads - 1)
    for i in range(owned // TILE):
        at = slice(i * TILE, (i + 1) * TILE)
        pout[:, at] = (pacc[1 - hd, :, at] + project(attn, heads - 1, 1 - hd, i * TILE)).astype(bf)
        send(pout.at[:, at], pin.at[:, at], ps.at[i], pr.at[i], to_pair)
    sum_lanes = jnp.zeros((rows, 128), f32)
    square_lanes = jnp.zeros((rows, 128), f32)
    for i in range(owned // TILE):
        at = slice(i * TILE, (i + 1) * TILE)
        mine = pacc[hd, :, at] + project(attn, heads - 1, hd, i * TILE)
        remote(pout.at[:, at], pin.at[:, at], ps.at[i], pr.at[i], to_pair).wait_recv()
        mine = mine + pin[:, at].astype(f32)
        hidden = (rbuf[:, at].astype(f32) + mfin[0:1, at] * mine).astype(bf)
        hidden_ref[:, at] = hidden
        wide = hidden.astype(f32)
        for c in range(0, TILE, 128):
            lane = wide[:, c : c + 128]
            sum_lanes += lane
            square_lanes += lane * lane
    stat[0] = sum_lanes
    stat[1] = square_lanes
    send(stat, stat_in, ss.at[1], sr.at[1], to_pair)
    remote(stat, stat_in, ss.at[1], sr.at[1], to_pair).wait_recv()
    mean = jnp.sum(stat[0] + stat_in[0], axis=1, keepdims=True) / D
    var = jnp.sum(stat[1] + stat_in[1], axis=1, keepdims=True) / D - mean * mean
    row_ref[0] = jnp.broadcast_to(mean, (rows, 128))
    row_ref[1] = jnp.broadcast_to(lax.rsqrt(var + 1e-06), (rows, 128))
    mod_ref[...] = mfin[...]
    for copy in sends:
        copy.wait_send()


def finish_kernel(hidden_ref, row_ref, mod_ref, hidden_out, mlp_out):
    hidden = hidden_ref[...]
    hidden_out[...] = hidden
    wide = hidden.astype(jnp.float32)
    mlp_out[...] = (
        (wide - row_ref[0, :, 0:1]) * row_ref[1, :, 0:1] * (1.0 + mod_ref[2:3, :]) + mod_ref[1:2, :]
    ).astype(jnp.bfloat16)


def fused_block(
    residual, query_proj, key_proj, value_proj, q_gain, k_gain, time_embed, time_proj, mod_table, out_weight
):
    rows, cols = query_proj.shape
    width = cols // LINE
    heads = width // HD
    owned = residual.shape[1]
    half_mod = mod_table.shape
    quarter = (half_mod[0], owned // PLANE)
    bf, f32 = jnp.bfloat16, jnp.float32
    dma = pltpu.SemaphoreType.DMA
    vmem = pl.BlockSpec(memory_space=pltpu.VMEM)
    hbm = pl.BlockSpec(memory_space=pl.ANY)
    blocks = LINE * PLANE
    count = heads * LINE * 2
    lines = time_proj.transpose(1, 0, 2)
    out = jax.ShapeDtypeStruct((rows, owned), bf)
    flat = pltpu.VMEM((rows, cols), bf)
    slab = pltpu.VMEM((heads, LINE, rows, HD), bf)
    lanes = pltpu.VMEM((2, rows, 128), f32)
    column = pltpu.VMEM((heads, LINE, rows, 1), f32)
    hidden, row, mod = pl.pallas_call(
        block_kernel,
        out_shape=(out, jax.ShapeDtypeStruct((2, rows, 128), f32), jax.ShapeDtypeStruct(half_mod, f32)),
        in_specs=[hbm, hbm, hbm, vmem, vmem, vmem, vmem, hbm, hbm, hbm],
        out_specs=(vmem, vmem, vmem),
        scratch_shapes=[
            flat, flat, flat, flat,
            pltpu.VMEM((heads, blocks, rows, HD), bf),
            pltpu.VMEM((heads, blocks, rows, HD), bf),
            slab, slab, slab,
            column, column,
            pltpu.VMEM((heads, LINE, rows, HD), f32),
            lanes, lanes, lanes,
            pltpu.VMEM((2,) + half_mod, f32),
            pltpu.VMEM(half_mod, f32),
            pltpu.VMEM(half_mod, f32),
            pltpu.VMEM((PLANE,) + quarter, f32),
            pltpu.VMEM((LINE + 1,) + quarter, f32),
            pltpu.VMEM(half_mod, f32),
            pltpu.VMEM(lines.shape, bf),
            pltpu.VMEM((heads, LINE * HD, 2 * owned), bf),
            pltpu.VMEM((rows, owned), bf),
            pltpu.VMEM((2, rows, owned), f32),
            pltpu.VMEM((rows, owned), bf),
            pltpu.VMEM((rows, owned), bf),
            lanes, lanes,
            dma((3 * heads + 1,)), dma((4 + heads * LINE,)), dma((9 * heads,)), dma((9 * heads,)),
        ]
        + [dma((count,))] * 8
        + [dma((3 * heads,))] * 2
        + [dma((10,))] * 2
        + [dma((owned // TILE,))] * 2
        + [dma((2,))] * 2,
        compiler_params=pltpu.CompilerParams(
            collective_id=0, has_side_effects=True, vmem_limit_bytes=60 * 1024 * 1024
        ),
    )(
        query_proj, key_proj, value_proj, q_gain, k_gain,
        time_embed.reshape(1, -1), mod_table, residual, lines, out_weight,
    )
    return pl.pallas_call(
        finish_kernel,
        out_shape=(out, out),
        in_specs=[vmem, vmem, vmem],
        out_specs=(vmem, vmem),
        compiler_params=pltpu.CompilerParams(vmem_limit_bytes=60 * 1024 * 1024),
    )(hidden, row, mod)


def accumulate(carry, queries, keys_block, values_block):
    count = keys_block.shape[0]
    heads_here = queries.shape[1]
    keys_three = keys_block.reshape(count, heads_here, HD)
    values_three = values_block.reshape(count, heads_here, HD).astype(jnp.float32)
    scores = jnp.einsum("thd,shd->ths", queries, keys_three, preferred_element_type=jnp.float32) * (
        1.0 / math.sqrt(HD)
    )
    top_old, total_old, summed = carry
    top_new = jnp.maximum(top_old, jnp.max(scores, axis=2))
    weights = jnp.exp(scores - top_new[:, :, None])
    total_new = jnp.sum(weights, axis=2)
    summed_new = jnp.einsum("ths,shd->thd", weights, values_three, precision=lax.Precision.HIGHEST)
    return (top_new, total_new, summed_new)


def shards(
    residual,
    query_proj,
    key_proj,
    value_proj,
    q_gain,
    k_gain,
    time_embed,
    time_proj,
    mod_table,
    out_weight,
):
    if (
        lax.axis_size("head") == 2
        and lax.axis_size("frame") == LINE * PLANE
        and query_proj.shape[1] % (LINE * HD) == 0
    ):
        return fused_block(
            residual, query_proj, key_proj, value_proj, q_gain, k_gain, time_embed, time_proj, mod_table, out_weight
        )
    emb = jax.nn.silu(time_embed)
    partial_mod = jnp.einsum(
        "r,rcd->cd", emb, time_proj.astype(jnp.float32), precision=lax.Precision.HIGHEST
    )
    width = mod_table.shape[1]
    summed_mod = lax.psum(partial_mod, ("frame", "head"))
    share = lax.dynamic_slice_in_dim(summed_mod, lax.axis_index("head") * width, width, 1)
    modulation = mod_table + share
    gate = modulation[0]
    shift = modulation[1]
    scale = modulation[2]
    tok_rows = query_proj.shape[0]
    heads_here = query_proj.shape[1] // HD
    query_wide = query_proj.astype(jnp.float32)
    key_wide = key_proj.astype(jnp.float32)
    total_q, total_k = lax.psum(
        (jnp.sum(query_wide * query_wide, axis=1), jnp.sum(key_wide * key_wide, axis=1)), "head"
    )
    query_rms = lax.rsqrt(total_q / (HEADS * HD) + 1e-06)
    key_rms = lax.rsqrt(total_k / (HEADS * HD) + 1e-06)
    queries = (
        (query_wide * query_rms[:, None] * q_gain)
        .astype(jnp.bfloat16)
        .reshape(tok_rows, heads_here, HD)
    )
    start_state = (
        jnp.full((tok_rows, heads_here), -1e30, jnp.float32),
        jnp.zeros((tok_rows, heads_here), jnp.float32),
        jnp.zeros((tok_rows, heads_here, HD), jnp.float32),
    )
    every_scale = lax.all_gather(key_rms, "frame", axis=0, tiled=True)
    keys_block = (
        lax.all_gather(key_proj, "frame", axis=0, tiled=True).astype(jnp.float32)
        * every_scale[:, None]
        * k_gain
    ).astype(jnp.bfloat16)
    top_final, total_final, summed_final = accumulate(
        start_state, queries, keys_block, lax.all_gather(value_proj, "frame", axis=0, tiled=True)
    )
    attn = (
        (summed_final / total_final[:, :, None])
        .astype(jnp.bfloat16)
        .reshape(tok_rows, heads_here * HD)
    )
    proj = (
        lax.psum_scatter(
            lax.dot_general(
                out_weight, attn, (((0,), (1,)), ((), ())), preferred_element_type=jnp.float32
            ).astype(jnp.bfloat16),
            "head",
            scatter_dimension=0,
            tiled=True,
        )
        .astype(jnp.float32)
        .T
    )
    hidden_out = (residual.astype(jnp.float32) + gate * proj).astype(jnp.bfloat16)
    hidden32 = lax.optimization_barrier(hidden_out).astype(jnp.float32)
    row_sum, row_squares = lax.psum(
        (jnp.sum(hidden32, axis=1), jnp.sum(hidden32 * hidden32, axis=1)), "head"
    )
    mean = row_sum[:, None] / D
    var = row_squares[:, None] / D - mean * mean
    mlp_input = ((hidden32 - mean) * lax.rsqrt(var + 1e-06) * (1.0 + scale) + shift).astype(
        jnp.bfloat16
    )
    return (hidden_out, mlp_input)


def solution(mesh):
    in_specs = (
        P("frame", "head"),
        P("frame", "head"),
        P("frame", "head"),
        P("frame", "head"),
        P("head"),
        P("head"),
        P(("frame", "head")),
        P(("frame", "head"), None, None),
        P(None, "head"),
        P("head", None),
    )
    out_specs = (P("frame", "head"), P("frame", "head"))
    return jax.shard_map(shards, mesh=mesh, in_specs=in_specs, out_specs=out_specs, check_vma=False)
```

```python
import math

import jax
import jax.numpy as jnp
from jax import lax
from jax.experimental import pallas as pl
from jax.experimental.pallas import tpu as pltpu
from jax.sharding import PartitionSpec as P

D = 5120
HEADS = 24
HD = 128
SHARP = math.log2(math.e) / math.sqrt(HD)


MESH = pl.DeviceIdType.MESH
PLANE = 4
LINE = 4
TILE = 512
FAR = (1, 3, 2)
KEY, VALUE, QUERY = 0, 1, 2
ORDER = (
    (VALUE, 0), (VALUE, 1), (KEY, 0), (QUERY, 0), (KEY, 1), (VALUE, 2), (KEY, 2), (QUERY, 1), (QUERY, 2),
)
WINDOW = 3
CHUNKS = 2
BEAT = 2.9
UNIT = 0.72
HOP = 4.0
HOP_Z = 4.0
ABSORB = 0.4
PROJECT = 1.0


def remote(src, dst, send, recv, device):
    return pltpu.make_async_remote_copy(
        src_ref=src, dst_ref=dst, send_sem=send, recv_sem=recv, device_id=device, device_id_type=MESH
    )


def queue_of(heads):
    if heads == 3:
        return list(ORDER)
    return [(b, h) for h in range(heads) for b in (VALUE, KEY, QUERY)]


def agenda(heads):
    queue = queue_of(heads)
    free = {"x": 0.0, "y": 0.0, "z": 0.0}
    soon, waiting, steps = [], {}, []

    def travel(link, now, size):
        free[link] = max(free[link], now) + size
        return free[link]

    def after(key, count, at, step):
        left, late = waiting.get(key, (count, 0.0))
        waiting[key] = (left - 1, max(late, at))
        if left == 1:
            soon.append((max(late, at), len(steps) + len(soon), step))

    def arrived(at, d, h, b):
        for link, name in (("x", "second_x"), ("y", "second_y")):
            soon.append((travel(link, at, UNIT) + HOP, 0, (name, d, h, b)))

    def run(now, step):
        name, of = step[0], step[1:]
        if name == "launch":
            b, h = of
            for d in FAR:
                at = travel("z", now, BEAT / 3) + HOP_Z
                soon.append((at, 0, ("query", d, h) if b == QUERY else ("first", d, h, b)))
            if b != QUERY:
                arrived(now, 0, h, b)
        elif name == "first":
            arrived(now, *of)
            landed(now, of[2], of[1])
        elif name == "query":
            d, h = of
            for e in (0,) + FAR:
                after(("absorb", e, h), 7, now, ("absorb", e, h))
            landed(now, QUERY, h)
        elif name in ("second_x", "second_y"):
            d, h, b = of
            at = travel("y" if name == "second_x" else "x", now, UNIT / 2) + HOP
            after(("absorb", d, h), 7, at, ("absorb", d, h))
        elif name == "absorb":
            d, h = of
            after(("last", h), LINE, now, ("flush", h))
        elif name == "flush":
            (h,) = of
            for d in FAR:
                at = travel("z", now, BEAT / 3) + HOP_Z
                after(("project", h), 3, at, ("project", h))
        elif name == "mod" and of[0] < 3:
            soon.append((now + (HOP + 0.5, HOP + 0.5, HOP_Z + 0.5)[of[0]] + (free["z"] - now if of[0] == 2 else 0.0), 0, ("mod", of[0] + 1)))

    def landed(now, b, h):
        n = queue.index((b, h)) + WINDOW
        if n < len(queue):
            after(("launch", n), 3, now, ("launch",) + queue[n])

    now = 0.0
    soon.append((5.0, 0, ("mod", 0)))
    for n, pair in enumerate(queue[:WINDOW]):
        soon.append((0.0 if n == 0 else 2.5, -1, ("launch",) + pair))
    cost = {"absorb": ABSORB, "project": PROJECT, "mod": 0.6, "launch": 0.2}
    while soon:
        soon.sort(key=lambda entry: (entry[0], entry[1]))
        ready = [entry for entry in soon if entry[0] <= now + 0.02]
        light = [entry for entry in ready if entry[2][0] not in ("absorb", "project", "mod")]
        work = [entry for entry in ready if entry[2][0] != "project"]
        pick = (light or work or ready or soon)[0]
        soon.remove(pick)
        now = max(now, pick[0]) + cost.get(pick[2][0], 0.04)
        run(now, pick[2])
        steps.append((now, pick[2]))
    return [step for now, step in steps if step[0] != "flush"][WINDOW:]


def block_kernel(
    q_hbm, k_hbm, v_hbm, qg_ref, kg_ref, te_ref, table_ref, res_hbm, proj_hbm, weight_hbm,
    hidden_hbm, row_ref, mod_hbm,
    qraw, kraw, qn, kn, kbuf, vbuf, qbuf, obuf, arecv, top, summed,
    squares, squares_in, rms, part, mpart, macc, mrs, mz, mfin, tbuf, wbuf, rbuf, pacc, pout, pin, hbuf, stat, stat_in,
    out_sem,    own_sem, load_sem, zs, zr, xs, xr, ys, yr, dxs, dxr, dys, dyr, os, orr, ms, mr, ps, pr, ss, sr,
):
    f32, bf = jnp.float32, jnp.bfloat16
    frames = LINE * PLANE
    f = lax.axis_index("frame")
    hd = lax.axis_index("head")
    z = lax.div(f, PLANE)
    x = lax.rem(f, 2)
    y = lax.rem(lax.div(f, 2), 2)
    step_x = 1 - 2 * x
    step_y = 2 - 4 * y
    to_x = {"frame": f + step_x}
    to_y = {"frame": f + step_y}
    to_xy = {"frame": f + step_x + step_y}
    to_pair = {"head": 1 - hd}
    rows, cols_all = qn.shape
    half = rows // 2
    width = cols_all // LINE
    heads = width // HD
    owned = hbuf.shape[1]
    quarter = owned // PLANE

    def later(d):
        return lax.rem(f + PLANE * d, frames)

    def earlier(d):
        return lax.rem(f + frames - PLANE * d, frames)

    def piece(ref, line, h):
        return ref.at[:, pl.ds(pl.multiple_of(line * width + h * HD, HD), HD)]

    def quarter_of(ref, spot):
        return ref.at[:, pl.ds(pl.multiple_of(spot * quarter, 128), quarter)]

    sends = []

    def send(src, dst, s, r, peer):
        copy = remote(src, dst, s, r, peer)
        copy.start()
        sends.append(copy)

    barrier = pltpu.get_barrier_semaphore()
    for d in range(1, LINE):
        pl.semaphore_signal(barrier, inc=1, device_id={"frame": later(d)}, device_id_type=MESH)
    for peer in (to_x, to_y, to_xy, to_pair):
        pl.semaphore_signal(barrier, inc=1, device_id=peer, device_id_type=MESH)

    raw = []
    for i, (src, dst) in enumerate(((q_hbm, qraw), (k_hbm, kraw))):
        raw.append(pltpu.make_async_copy(src, dst, load_sem.at[i]))
        raw[i].start()
    loads = [pltpu.make_async_copy(proj_hbm, tbuf, load_sem.at[2])]
    loads.append(pltpu.make_async_copy(res_hbm, rbuf, load_sem.at[3]))
    for h in range(heads):
        for j in range(LINE):
            at = pl.ds(j * width + h * HD, HD)
            loads.append(
                pltpu.make_async_copy(weight_hbm.at[at], wbuf.at[h, pl.ds(j * HD, HD)], load_sem.at[4 + h * LINE + j])
            )
    for i, ref in enumerate((qraw, kraw)):
        raw[i].wait()
        lanes = jnp.zeros((rows, 128), f32)
        for c in range(0, cols_all, 128):
            wide = ref[:, c : c + 128].astype(f32)
            lanes += wide * wide
        squares[i] = lanes
    pl.semaphore_wait(barrier, LINE + 3)

    bufs = (kbuf, vbuf)
    own = {}

    def number(h, d, b):
        return (h * LINE + d) * 2 + b

    def send_line(b, h, src, dst):
        for d in FAR:
            peer = later(d)
            n = (b * heads + h) * 3 + d - 1
            send(piece(src, lax.div(peer, PLANE), h), dst, zs.at[n], zr.at[n], {"frame": peer})

    def send_own(b, h, src, dst):
        mine = piece(src, z, h)
        if b != QUERY:
            n = number(h, 0, b)
            send(mine, dst, xs.at[n], xr.at[n], to_x)
            send(mine, dst, ys.at[n], yr.at[n], to_y)
        own[b, h] = pltpu.make_async_copy(mine, dst, own_sem.at[b * heads + h])
        own[b, h].start()

    def launch(b, h):
        if b == VALUE:
            src, dst = v_hbm, vbuf.at[h, f]
        else:
            i, ref, gain, src, dst = (
                (1, kraw, kg_ref, kn, kbuf.at[h, f]) if b == KEY else (0, qraw, qg_ref, qn, qbuf.at[h, z])
            )
            for j in range(LINE):
                at = slice(j * width + h * HD, j * width + (h + 1) * HD)
                src[:, at] = (ref[:, at].astype(f32) * rms[i, :, 0:1] * gain[at].reshape(1, HD)).astype(bf)
        send_line(b, h, src, dst)
        send_own(b, h, src, dst)

    send(squares, squares_in, ss.at[0], sr.at[0], to_pair)
    launch(*queue_of(heads)[0])
    for copy in loads:
        copy.start()

    remote(squares, squares_in, ss.at[0], sr.at[0], to_pair).wait_recv()
    for i in range(2):
        sums = jnp.sum(squares[i] + squares_in[i], axis=1, keepdims=True)
        rms[i] = jnp.broadcast_to(lax.rsqrt(sums / (HEADS * HD) + 1e-06), (rows, 128))
    for b, h in queue_of(heads)[1:WINDOW]:
        launch(b, h)

    def first(d, h, b):
        n = number(h, d, b)
        m = (b * heads + h) * 3 + d - 1
        at = earlier(d)
        block = bufs[b].at[h, at]
        remote(block, block, zs.at[m], zr.at[m], {"frame": at}).wait_recv()
        send(block, block, xs.at[n], xr.at[n], to_x)
        send(block, block, ys.at[n], yr.at[n], to_y)

    def second_x(d, h, b):
        n = number(h, d, b)
        block = bufs[b].at[h, earlier(d) + step_x]
        remote(block, block, xs.at[n], xr.at[n], to_x).wait_recv()
        low = block.at[pl.ds(half, half)]
        send(low, low, dys.at[n], dyr.at[n], to_y)

    def second_y(d, h, b):
        n = number(h, d, b)
        block = bufs[b].at[h, earlier(d) + step_y]
        remote(block, block, ys.at[n], yr.at[n], to_y).wait_recv()
        high = block.at[pl.ds(0, half)]
        send(high, high, dxs.at[n], dxr.at[n], to_x)

    def third(d, h, b):
        n = number(h, d, b)
        block = bufs[b].at[h, earlier(d) + step_x + step_y]
        high = block.at[pl.ds(0, half)]
        remote(high, high, dxs.at[n], dxr.at[n], to_x).wait_recv()
        low = block.at[pl.ds(half, half)]
        remote(low, low, dys.at[n], dyr.at[n], to_y).wait_recv()

    def query(d, h):
        m = (QUERY * heads + h) * 3 + d - 1
        block = qbuf.at[h, lax.div(earlier(d), PLANE)]
        remote(block, block, zs.at[m], zr.at[m], {"frame": earlier(d)}).wait_recv()

    def absorb(d, h):
        opening, closing = done[h] == 0, done[h] == LINE - 1
        done[h] += 1
        if d == 0:
            own[KEY, h].wait()
            own[VALUE, h].wait()
        if opening:
            own[QUERY, h].wait()
        third(d, h, KEY)
        third(d, h, VALUE)
        base = pl.multiple_of(lax.div(earlier(d), PLANE) * PLANE, PLANE)
        group = pl.ds(base, PLANE)

        def block_of(i, carry):
            keys = kbuf[h, group].reshape(PLANE * rows, HD)
            values = vbuf[h, group].reshape(PLANE * rows, HD)
            values = jnp.concatenate([values, jnp.ones((PLANE * rows, HD), bf)], axis=1)
            scores = lax.dot_general(qbuf[h, i], keys, (((1,), (1,)), ((), ())), preferred_element_type=f32)
            peak = jnp.broadcast_to(jnp.max(scores, axis=1, keepdims=True) * SHARP, (rows, HD))
            if not opening:
                old = top[h, i]
                peak = jnp.maximum(old, peak)
                fade = jnp.exp2(old - peak)
            weights = [
                jnp.exp2(scores[:, c : c + HD] * SHARP - peak).astype(bf) for c in range(0, PLANE * rows, HD)
            ]
            mixed = jnp.dot(jnp.concatenate(weights, axis=1), values, preferred_element_type=f32)
            if not opening:
                mixed = mixed + jnp.concatenate([fade, fade], axis=1) * summed[h, i]
            if closing:
                obuf[h, i] = (mixed[:, :HD] / mixed[:, HD:]).astype(bf)
            else:
                top[h, i] = peak
                summed[h, i] = mixed
            return carry

        lax.fori_loop(0, LINE, block_of, 0, unroll=True)
        if closing:
            for e in FAR:
                n = h * 3 + e - 1
                send(
                    obuf.at[h, lax.div(later(e), PLANE)], arecv.at[h, z],
                    os.at[n], orr.at[n], {"frame": later(e)},
                )
            arecv[h, z] = obuf[h, z]

    spot = lax.rem(f, PLANE)
    plane = ((to_x, spot + step_x), (to_y, spot + step_y), (to_xy, spot + step_x + step_y))

    def mod(stage):
        if stage == 0:
            loads[0].wait()
            t = te_ref[...]
            emb = t / (1.0 + jnp.exp(-t))
            high = emb.astype(bf).astype(f32)
            middle = (emb - high).astype(bf).astype(f32)
            low = emb - high - middle
            row = lax.broadcasted_iota(jnp.int32, (8, emb.shape[1]), 0)
            split = jnp.where(row == 0, high, jnp.where(row == 1, middle, jnp.where(row == 2, low, 0.0)))
            split = split.astype(bf)
            for c in range(3):
                for side in range(2):
                    term = jnp.dot(
                        split, tbuf[c, :, side * owned : (side + 1) * owned], preferred_element_type=f32
                    )
                    part[side, c : c + 1, :] = jnp.sum(term, axis=0, keepdims=True)
            send(part.at[1 - hd], mpart, ms.at[0], mr.at[0], to_pair)
        elif stage == 1:
            remote(part.at[1 - hd], mpart, ms.at[0], mr.at[0], to_pair).wait_recv()
            macc[...] = part[hd] + mpart[...]
            for i, (peer, theirs) in enumerate(plane):
                send(quarter_of(macc, theirs), mrs.at[i + 1], ms.at[1 + i], mr.at[1 + i], peer)
            keep = pltpu.make_async_copy(quarter_of(macc, spot), mrs.at[0], own_sem.at[3 * heads])
            keep.start()
            keep.wait()
        elif stage == 2:
            for i, (peer, theirs) in enumerate(plane):
                remote(mrs.at[i + 1], mrs.at[i + 1], ms.at[1 + i], mr.at[1 + i], peer).wait_recv()
            mz[0] = (mrs[0] + mrs[1]) + (mrs[2] + mrs[3])
            for d in range(1, LINE):
                send(mz.at[0], mz.at[d], ms.at[3 + d], mr.at[3 + d], {"frame": later(d)})
        elif stage == 3:
            for d in range(1, LINE):
                remote(mz.at[0], mz.at[d], ms.at[3 + d], mr.at[3 + d], {"frame": earlier(d)}).wait_recv()
            mz[LINE] = (mz[0] + mz[2]) + (mz[1] + mz[3])
            mine = quarter_of(mfin, spot)
            for i, (peer, theirs) in enumerate(plane):
                send(mz.at[LINE], mine, ms.at[7 + i], mr.at[7 + i], peer)
            keep = pltpu.make_async_copy(mz.at[LINE], mine, own_sem.at[3 * heads])
            keep.start()
            keep.wait()
        else:
            for i, (peer, theirs) in enumerate(plane):
                block = quarter_of(mfin, theirs)
                remote(block, block, ms.at[7 + i], mr.at[7 + i], peer).wait_recv()
            mfin[...] = mfin[...] + table_ref[...]

    def gathered(h):
        for d in range(1, LINE):
            n = h * 3 + d - 1
            block = arecv.at[h, lax.div(earlier(d), PLANE)]
            remote(block, block, os.at[n], orr.at[n], {"frame": earlier(d)}).wait_recv()
        for copy in loads[2 + h * LINE : 2 + (h + 1) * LINE]:
            copy.wait()
        return jnp.concatenate([arecv[h, j] for j in range(LINE)], axis=1)

    def share_of(attn, h, side, at):
        begin = pl.multiple_of(side * owned + at, 128)
        return jnp.dot(attn, wbuf[h, :, pl.ds(begin, TILE)], preferred_element_type=f32)

    fresh = [True]

    def project(h):
        attn = gathered(h)
        for side in range(2):
            for i in range(owned // TILE):
                at = slice(i * TILE, (i + 1) * TILE)
                share = share_of(attn, h, side, i * TILE)
                pacc[side, :, at] = share if fresh[0] else pacc[side, :, at] + share
        fresh[0] = False

    done = [0] * heads
    todo = {
        "launch": launch, "query": query, "first": first, "second_x": second_x, "second_y": second_y,
        "absorb": absorb, "mod": mod, "project": project,
    }
    plan = agenda(heads)
    last = plan[-1][1]
    for name, *of in plan[:-1]:
        todo[name](*of)
    mod(4)
    outs = [pltpu.make_async_copy(mfin, mod_hbm, out_sem.at[owned // TILE])]
    outs[0].start()
    loads[1].wait()
    for copy in sends[: -3]:
        copy.wait_send()
    del sends[: -3]
    attn = gathered(last)
    for i in range(owned // TILE):
        at = slice(i * TILE, (i + 1) * TILE)
        pout[:, at] = (pacc[1 - hd, :, at] + share_of(attn, last, 1 - hd, i * TILE)).astype(bf)
        send(pout.at[:, at], pin.at[:, at], ps.at[i], pr.at[i], to_pair)
    sum_lanes = jnp.zeros((rows, 128), f32)
    square_lanes = jnp.zeros((rows, 128), f32)
    for i in range(owned // TILE):
        at = slice(i * TILE, (i + 1) * TILE)
        mine = pacc[hd, :, at] + share_of(attn, last, hd, i * TILE)
        remote(pout.at[:, at], pin.at[:, at], ps.at[i], pr.at[i], to_pair).wait_recv()
        mine = mine + pin[:, at].astype(f32)
        hidden = (rbuf[:, at].astype(f32) + mfin[0:1, at] * mine).astype(bf)
        hbuf[:, at] = hidden
        outs.append(pltpu.make_async_copy(hbuf.at[:, at], hidden_hbm.at[:, at], out_sem.at[i]))
        outs[-1].start()
        wide = hidden.astype(f32)
        for c in range(0, TILE, 128):
            lane = wide[:, c : c + 128]
            sum_lanes += lane
            square_lanes += lane * lane
    stat[0] = sum_lanes
    stat[1] = square_lanes
    send(stat, stat_in, ss.at[1], sr.at[1], to_pair)
    remote(stat, stat_in, ss.at[1], sr.at[1], to_pair).wait_recv()
    mean = jnp.sum(stat[0] + stat_in[0], axis=1, keepdims=True) / D
    var = jnp.sum(stat[1] + stat_in[1], axis=1, keepdims=True) / D - mean * mean
    row_ref[0] = jnp.broadcast_to(mean, (rows, 128))
    row_ref[1] = jnp.broadcast_to(lax.rsqrt(var + 1e-06), (rows, 128))
    for copy in outs:
        copy.wait()
    for copy in sends:
        copy.wait_send()


def finish_kernel(hidden_hbm, row_hbm, mod_hbm, hidden_out, mlp_out, hbuf, mbuf, row, mod, sem, in_sem, out_sem, mlp_sem):
    rows, owned = hbuf.shape
    step = rows // CHUNKS
    small = [pltpu.make_async_copy(row_hbm, row, sem.at[0]), pltpu.make_async_copy(mod_hbm, mod, sem.at[1])]
    parts = [pl.ds(i * step, step) for i in range(CHUNKS)]
    loads = [pltpu.make_async_copy(hidden_hbm.at[at], hbuf.at[at], in_sem.at[i]) for i, at in enumerate(parts)]
    for copy in small + loads:
        copy.start()
    for copy in small:
        copy.wait()
    outs = []
    for i, at in enumerate(parts):
        loads[i].wait()
        outs.append(pltpu.make_async_copy(hbuf.at[at], hidden_out.at[at], out_sem.at[i]))
        outs[-1].start()
        for c in range(0, owned, 128):
            lane = slice(c, c + 128)
            wide = hbuf[at, lane].astype(jnp.float32)
            mbuf[at, lane] = (
                (wide - row[0, at]) * row[1, at] * (1.0 + mod[2:3, lane]) + mod[1:2, lane]
            ).astype(jnp.bfloat16)
        outs.append(pltpu.make_async_copy(mbuf.at[at], mlp_out.at[at], mlp_sem.at[i]))
        outs[-1].start()
    for copy in outs:
        copy.wait()


def fused_block(
    residual, query_proj, key_proj, value_proj, q_gain, k_gain, time_embed, time_proj, mod_table, out_weight
):
    rows, cols = query_proj.shape
    width = cols // LINE
    heads = width // HD
    owned = residual.shape[1]
    half_mod = mod_table.shape
    quarter = (half_mod[0], owned // PLANE)
    bf, f32 = jnp.bfloat16, jnp.float32
    dma = pltpu.SemaphoreType.DMA
    vmem = pl.BlockSpec(memory_space=pltpu.VMEM)
    hbm = pl.BlockSpec(memory_space=pl.ANY)
    blocks = LINE * PLANE
    count = heads * LINE * 2
    lines = time_proj.transpose(1, 0, 2)
    out = jax.ShapeDtypeStruct((rows, owned), bf)
    flat = pltpu.VMEM((rows, cols), bf)
    slab = pltpu.VMEM((heads, LINE, rows, HD), bf)
    lanes = pltpu.VMEM((2, rows, 128), f32)
    hidden, row, mod = pl.pallas_call(
        block_kernel,
        out_shape=(out, jax.ShapeDtypeStruct((2, rows, 128), f32), jax.ShapeDtypeStruct(half_mod, f32)),
        in_specs=[hbm, hbm, hbm, vmem, vmem, vmem, vmem, hbm, hbm, hbm],
        out_specs=(hbm, vmem, hbm),
        scratch_shapes=[
            flat, flat, flat, flat,
            pltpu.VMEM((heads, blocks, rows, HD), bf),
            pltpu.VMEM((heads, blocks, rows, HD), bf),
            slab, slab, slab,
            pltpu.VMEM((heads, LINE, rows, HD), f32),
            pltpu.VMEM((heads, LINE, rows, 2 * HD), f32),
            lanes, lanes, lanes,
            pltpu.VMEM((2,) + half_mod, f32),
            pltpu.VMEM(half_mod, f32),
            pltpu.VMEM(half_mod, f32),
            pltpu.VMEM((PLANE,) + quarter, f32),
            pltpu.VMEM((LINE + 1,) + quarter, f32),
            pltpu.VMEM(half_mod, f32),
            pltpu.VMEM(lines.shape, bf),
            pltpu.VMEM((heads, LINE * HD, 2 * owned), bf),
            pltpu.VMEM((rows, owned), bf),
            pltpu.VMEM((2, rows, owned), f32),
            pltpu.VMEM((rows, owned), bf),
            pltpu.VMEM((rows, owned), bf),
            pltpu.VMEM((rows, owned), bf),
            lanes, lanes,
            dma((owned // TILE + 1,)),
            dma((3 * heads + 1,)), dma((4 + heads * LINE,)), dma((9 * heads,)), dma((9 * heads,)),
        ]
        + [dma((count,))] * 8
        + [dma((3 * heads,))] * 2
        + [dma((10,))] * 2
        + [dma((owned // TILE,))] * 2
        + [dma((2,))] * 2,
        compiler_params=pltpu.CompilerParams(
            collective_id=0, has_side_effects=True, vmem_limit_bytes=60 * 1024 * 1024
        ),
    )(
        query_proj, key_proj, value_proj, q_gain, k_gain,
        time_embed.reshape(1, -1), mod_table, residual, lines, out_weight,
    )
    return pl.pallas_call(
        finish_kernel,
        out_shape=(out, out),
        in_specs=[hbm, hbm, hbm],
        out_specs=(hbm, hbm),
        scratch_shapes=[
            pltpu.VMEM((rows, owned), bf),
            pltpu.VMEM((rows, owned), bf),
            pltpu.VMEM((2, rows, 128), f32),
            pltpu.VMEM(half_mod, f32),
            dma((2,)), dma((CHUNKS,)), dma((CHUNKS,)), dma((CHUNKS,)),
        ],
        compiler_params=pltpu.CompilerParams(vmem_limit_bytes=60 * 1024 * 1024),
    )(hidden, row, mod)


def accumulate(carry, queries, keys_block, values_block):
    count = keys_block.shape[0]
    heads_here = queries.shape[1]
    keys_three = keys_block.reshape(count, heads_here, HD)
    values_three = values_block.reshape(count, heads_here, HD).astype(jnp.float32)
    scores = jnp.einsum("thd,shd->ths", queries, keys_three, preferred_element_type=jnp.float32) * (
        1.0 / math.sqrt(HD)
    )
    top_old, total_old, summed = carry
    top_new = jnp.maximum(top_old, jnp.max(scores, axis=2))
    weights = jnp.exp(scores - top_new[:, :, None])
    total_new = jnp.sum(weights, axis=2)
    summed_new = jnp.einsum("ths,shd->thd", weights, values_three, precision=lax.Precision.HIGHEST)
    return (top_new, total_new, summed_new)


def shards(
    residual,
    query_proj,
    key_proj,
    value_proj,
    q_gain,
    k_gain,
    time_embed,
    time_proj,
    mod_table,
    out_weight,
):
    if (
        lax.axis_size("head") == 2
        and lax.axis_size("frame") == LINE * PLANE
        and query_proj.shape[1] % (LINE * HD) == 0
    ):
        return fused_block(
            residual, query_proj, key_proj, value_proj, q_gain, k_gain, time_embed, time_proj, mod_table, out_weight
        )
    emb = jax.nn.silu(time_embed)
    partial_mod = jnp.einsum(
        "r,rcd->cd", emb, time_proj.astype(jnp.float32), precision=lax.Precision.HIGHEST
    )
    width = mod_table.shape[1]
    summed_mod = lax.psum(partial_mod, ("frame", "head"))
    share = lax.dynamic_slice_in_dim(summed_mod, lax.axis_index("head") * width, width, 1)
    modulation = mod_table + share
    gate = modulation[0]
    shift = modulation[1]
    scale = modulation[2]
    tok_rows = query_proj.shape[0]
    heads_here = query_proj.shape[1] // HD
    query_wide = query_proj.astype(jnp.float32)
    key_wide = key_proj.astype(jnp.float32)
    total_q, total_k = lax.psum(
        (jnp.sum(query_wide * query_wide, axis=1), jnp.sum(key_wide * key_wide, axis=1)), "head"
    )
    query_rms = lax.rsqrt(total_q / (HEADS * HD) + 1e-06)
    key_rms = lax.rsqrt(total_k / (HEADS * HD) + 1e-06)
    queries = (
        (query_wide * query_rms[:, None] * q_gain)
        .astype(jnp.bfloat16)
        .reshape(tok_rows, heads_here, HD)
    )
    start_state = (
        jnp.full((tok_rows, heads_here), -1e30, jnp.float32),
        jnp.zeros((tok_rows, heads_here), jnp.float32),
        jnp.zeros((tok_rows, heads_here, HD), jnp.float32),
    )
    every_scale = lax.all_gather(key_rms, "frame", axis=0, tiled=True)
    keys_block = (
        lax.all_gather(key_proj, "frame", axis=0, tiled=True).astype(jnp.float32)
        * every_scale[:, None]
        * k_gain
    ).astype(jnp.bfloat16)
    top_final, total_final, summed_final = accumulate(
        start_state, queries, keys_block, lax.all_gather(value_proj, "frame", axis=0, tiled=True)
    )
    attn = (
        (summed_final / total_final[:, :, None])
        .astype(jnp.bfloat16)
        .reshape(tok_rows, heads_here * HD)
    )
    proj = (
        lax.psum_scatter(
            lax.dot_general(
                out_weight, attn, (((0,), (1,)), ((), ())), preferred_element_type=jnp.float32
            ).astype(jnp.bfloat16),
            "head",
            scatter_dimension=0,
            tiled=True,
        )
        .astype(jnp.float32)
        .T
    )
    hidden_out = (residual.astype(jnp.float32) + gate * proj).astype(jnp.bfloat16)
    hidden32 = lax.optimization_barrier(hidden_out).astype(jnp.float32)
    row_sum, row_squares = lax.psum(
        (jnp.sum(hidden32, axis=1), jnp.sum(hidden32 * hidden32, axis=1)), "head"
    )
    mean = row_sum[:, None] / D
    var = row_squares[:, None] / D - mean * mean
    mlp_input = ((hidden32 - mean) * lax.rsqrt(var + 1e-06) * (1.0 + scale) + shift).astype(
        jnp.bfloat16
    )
    return (hidden_out, mlp_input)


def solution(mesh):
    in_specs = (
        P("frame", "head"),
        P("frame", "head"),
        P("frame", "head"),
        P("frame", "head"),
        P("head"),
        P("head"),
        P(("frame", "head")),
        P(("frame", "head"), None, None),
        P(None, "head"),
        P("head", None),
    )
    out_specs = (P("frame", "head"), P("frame", "head"))
    return jax.shard_map(shards, mesh=mesh, in_specs=in_specs, out_specs=out_specs, check_vma=False)
```

```python
import math

import jax
import jax.numpy as jnp
from jax import lax
from jax.experimental import pallas as pl
from jax.experimental.pallas import tpu as pltpu
from jax.sharding import PartitionSpec as P

D = 5120
HEADS = 24
HD = 128
SHARP = math.log2(math.e) / math.sqrt(HD)


MESH = pl.DeviceIdType.MESH
PLANE = 4
LINE = 4
TILE = 512
FAR = (1, 3, 2)
KEY, VALUE, QUERY = 0, 1, 2
ORDER = (
    (VALUE, 0), (VALUE, 1), (KEY, 0), (QUERY, 0), (KEY, 1), (VALUE, 2), (KEY, 2), (QUERY, 1), (QUERY, 2),
)
WINDOW = 4
CHUNKS = 2
BEAT = 2.9
UNIT = 0.72
HOP = 3.5
HOP_Z = 3.5
ABSORB = 0.4
PROJECT = 0.5


def remote(src, dst, send, recv, device):
    return pltpu.make_async_remote_copy(
        src_ref=src, dst_ref=dst, send_sem=send, recv_sem=recv, device_id=device, device_id_type=MESH
    )


def queue_of(heads):
    if heads == 3:
        return list(ORDER)
    return [(b, h) for h in range(heads) for b in (VALUE, KEY, QUERY)]


def agenda(heads):
    queue = queue_of(heads)
    free = {"x": 0.0, "y": 0.0, "z": 0.0}
    soon, waiting, steps = [], {}, []

    def travel(link, now, size):
        free[link] = max(free[link], now) + size
        return free[link]

    def after(key, count, at, step):
        left, late = waiting.get(key, (count, 0.0))
        waiting[key] = (left - 1, max(late, at))
        if left == 1:
            soon.append((max(late, at), len(steps) + len(soon), step))

    def arrived(at, d, h, b):
        for link, name in (("x", "second_x"), ("y", "second_y")):
            soon.append((travel(link, at, UNIT) + HOP, 0, (name, d, h, b)))

    def run(now, step):
        name, of = step[0], step[1:]
        if name == "launch":
            b, h = of
            for d in FAR:
                at = travel("z", now, BEAT / 3) + HOP_Z
                soon.append((at, 0, ("query", d, h) if b == QUERY else ("first", d, h, b)))
            if b != QUERY:
                arrived(now, 0, h, b)
        elif name == "first":
            arrived(now, *of)
            landed(now, of[2], of[1])
        elif name == "query":
            d, h = of
            for e in (0,) + FAR:
                after(("absorb", e, h), 7, now, ("absorb", e, h))
            landed(now, QUERY, h)
        elif name in ("second_x", "second_y"):
            d, h, b = of
            at = travel("y" if name == "second_x" else "x", now, UNIT / 2) + HOP
            after(("absorb", d, h), 7, at, ("absorb", d, h))
        elif name == "absorb":
            d, h = of
            after(("last", h), LINE, now, ("flush", h))
        elif name == "flush":
            (h,) = of
            for d in FAR:
                at = travel("z", now, BEAT / 3) + HOP_Z
                after(("project", h), 3, at, ("project", h))
        elif name == "project":
            soon.append((now + HOP, 0, ("merge",) + of))
        elif name == "mod" and of[0] < 3:
            soon.append((now + (HOP + 0.5, HOP + 0.5, HOP_Z + 0.5)[of[0]] + (free["z"] - now if of[0] == 2 else 0.0), 0, ("mod", of[0] + 1)))

    def landed(now, b, h):
        n = queue.index((b, h)) + WINDOW
        if n < len(queue):
            after(("launch", n), 3, now, ("launch",) + queue[n])

    now = 0.0
    soon.append((5.0, 0, ("mod", 0)))
    for n, pair in enumerate(queue[:WINDOW]):
        soon.append((0.0 if n == 0 else 2.5, -1, ("launch",) + pair))
    cost = {"absorb": ABSORB, "project": PROJECT, "merge": PROJECT, "mod": 0.6, "launch": 0.2}
    while soon:
        soon.sort(key=lambda entry: (entry[0], entry[1]))
        ready = [entry for entry in soon if entry[0] <= now + 0.02]
        light = [entry for entry in ready if entry[2][0] not in ("absorb", "project", "merge", "mod")]
        work = [entry for entry in ready if entry[2][0] not in ("project", "merge")]
        pick = (light or work or ready or soon)[0]
        soon.remove(pick)
        now = max(now, pick[0]) + cost.get(pick[2][0], 0.04)
        run(now, pick[2])
        steps.append((now, pick[2]))
    return [step for now, step in steps if step[0] != "flush"][WINDOW:]


def block_kernel(
    q_hbm, k_hbm, v_hbm, qg_ref, kg_ref, te_ref, table_ref, res_hbm, proj_hbm, weight_hbm,
    hidden_hbm, row_ref, mod_hbm,
    qraw, kraw, qn, kn, kbuf, vbuf, qbuf, obuf, arecv, top, summed,
    squares, squares_in, rms, part, mpart, macc, mrs, mz, mfin, tbuf, wown, wother, aother, rbuf, pacc, hbuf, stat, stat_in,
    out_sem,    own_sem, load_sem, zs, zr, xs, xr, ys, yr, dxs, dxr, dys, dyr, os, orr, ms, mr, ws, wr, fs, fr, ss, sr,
):
    f32, bf = jnp.float32, jnp.bfloat16
    frames = LINE * PLANE
    f = lax.axis_index("frame")
    hd = lax.axis_index("head")
    z = lax.div(f, PLANE)
    x = lax.rem(f, 2)
    y = lax.rem(lax.div(f, 2), 2)
    step_x = 1 - 2 * x
    step_y = 2 - 4 * y
    to_x = {"frame": f + step_x}
    to_y = {"frame": f + step_y}
    to_xy = {"frame": f + step_x + step_y}
    to_pair = {"head": 1 - hd}
    rows, cols_all = qn.shape
    half = rows // 2
    width = cols_all // LINE
    heads = width // HD
    owned = hbuf.shape[1]
    quarter = owned // PLANE

    def later(d):
        return lax.rem(f + PLANE * d, frames)

    def earlier(d):
        return lax.rem(f + frames - PLANE * d, frames)

    def piece(ref, line, h):
        return ref.at[:, pl.ds(pl.multiple_of(line * width + h * HD, HD), HD)]

    def quarter_of(ref, spot):
        return ref.at[:, pl.ds(pl.multiple_of(spot * quarter, 128), quarter)]

    sends, late = [], []
    plan = agenda(heads)
    last = plan[-1][1]

    def send(src, dst, s, r, peer, among=sends):
        copy = remote(src, dst, s, r, peer)
        copy.start()
        among.append(copy)

    barrier = pltpu.get_barrier_semaphore()
    for d in range(1, LINE):
        pl.semaphore_signal(barrier, inc=1, device_id={"frame": later(d)}, device_id_type=MESH)
    for peer in (to_x, to_y, to_xy, to_pair):
        pl.semaphore_signal(barrier, inc=1, device_id=peer, device_id_type=MESH)

    raw = []
    for i, (src, dst) in enumerate(((q_hbm, qraw), (k_hbm, kraw))):
        raw.append(pltpu.make_async_copy(src, dst, load_sem.at[i]))
        raw[i].start()
    loads = [pltpu.make_async_copy(proj_hbm, tbuf, load_sem.at[2])]
    loads.append(pltpu.make_async_copy(res_hbm, rbuf, load_sem.at[3]))
    def weight(h, j, side):
        columns = pl.ds(pl.multiple_of(side * owned, 128), owned)
        return weight_hbm.at[pl.ds(j * width + h * HD, HD), columns], pl.ds(j * HD, HD)

    for h in range(heads):
        for j in range(LINE):
            block, at = weight(h, j, hd)
            loads.append(pltpu.make_async_copy(block, wown.at[h, at], load_sem.at[4 + h * LINE + j]))
    for i, ref in enumerate((qraw, kraw)):
        raw[i].wait()
        lanes = jnp.zeros((rows, 128), f32)
        for c in range(0, cols_all, 128):
            wide = ref[:, c : c + 128].astype(f32)
            lanes += wide * wide
        squares[i] = lanes
    pl.semaphore_wait(barrier, LINE + 3)

    bufs = (kbuf, vbuf)
    own = {}

    def number(h, d, b):
        return (h * LINE + d) * 2 + b

    def send_line(b, h, src, dst):
        for d in FAR:
            peer = later(d)
            n = (b * heads + h) * 3 + d - 1
            send(piece(src, lax.div(peer, PLANE), h), dst, zs.at[n], zr.at[n], {"frame": peer})

    def send_own(b, h, src, dst):
        mine = piece(src, z, h)
        if b != QUERY:
            n = number(h, 0, b)
            send(mine, dst, xs.at[n], xr.at[n], to_x)
            send(mine, dst, ys.at[n], yr.at[n], to_y)
        own[b, h] = pltpu.make_async_copy(mine, dst, own_sem.at[b * heads + h])
        own[b, h].start()

    def launch(b, h):
        if b == VALUE:
            src, dst = v_hbm, vbuf.at[h, f]
        else:
            i, ref, gain, src, dst = (
                (1, kraw, kg_ref, kn, kbuf.at[h, f]) if b == KEY else (0, qraw, qg_ref, qn, qbuf.at[h, z])
            )
            for j in range(LINE):
                at = slice(j * width + h * HD, j * width + (h + 1) * HD)
                src[:, at] = (ref[:, at].astype(f32) * rms[i, :, 0:1] * gain[at].reshape(1, HD)).astype(bf)
        send_line(b, h, src, dst)
        send_own(b, h, src, dst)

    send(squares, squares_in, ss.at[0], sr.at[0], to_pair)
    launch(*queue_of(heads)[0])
    for copy in loads:
        copy.start()

    remote(squares, squares_in, ss.at[0], sr.at[0], to_pair).wait_recv()
    for i in range(2):
        sums = jnp.sum(squares[i] + squares_in[i], axis=1, keepdims=True)
        rms[i] = jnp.broadcast_to(lax.rsqrt(sums / (HEADS * HD) + 1e-06), (rows, 128))
    for b, h in queue_of(heads)[1:WINDOW]:
        launch(b, h)

    def first(d, h, b):
        n = number(h, d, b)
        m = (b * heads + h) * 3 + d - 1
        at = earlier(d)
        block = bufs[b].at[h, at]
        remote(block, block, zs.at[m], zr.at[m], {"frame": at}).wait_recv()
        send(block, block, xs.at[n], xr.at[n], to_x)
        send(block, block, ys.at[n], yr.at[n], to_y)

    def second_x(d, h, b):
        n = number(h, d, b)
        block = bufs[b].at[h, earlier(d) + step_x]
        remote(block, block, xs.at[n], xr.at[n], to_x).wait_recv()
        low = block.at[pl.ds(half, half)]
        send(low, low, dys.at[n], dyr.at[n], to_y)

    def second_y(d, h, b):
        n = number(h, d, b)
        block = bufs[b].at[h, earlier(d) + step_y]
        remote(block, block, ys.at[n], yr.at[n], to_y).wait_recv()
        high = block.at[pl.ds(0, half)]
        send(high, high, dxs.at[n], dxr.at[n], to_x)

    def third(d, h, b):
        n = number(h, d, b)
        block = bufs[b].at[h, earlier(d) + step_x + step_y]
        high = block.at[pl.ds(0, half)]
        remote(high, high, dxs.at[n], dxr.at[n], to_x).wait_recv()
        low = block.at[pl.ds(half, half)]
        remote(low, low, dys.at[n], dyr.at[n], to_y).wait_recv()

    def query(d, h):
        m = (QUERY * heads + h) * 3 + d - 1
        block = qbuf.at[h, lax.div(earlier(d), PLANE)]
        remote(block, block, zs.at[m], zr.at[m], {"frame": earlier(d)}).wait_recv()

    def absorb(d, h):
        opening, closing = done[h] == 0, done[h] == LINE - 1
        done[h] += 1
        if d == 0:
            own[KEY, h].wait()
            own[VALUE, h].wait()
        if opening:
            own[QUERY, h].wait()
        third(d, h, KEY)
        third(d, h, VALUE)
        base = pl.multiple_of(lax.div(earlier(d), PLANE) * PLANE, PLANE)
        group = pl.ds(base, PLANE)

        def block_of(i, carry):
            keys = kbuf[h, group].reshape(PLANE * rows, HD)
            values = vbuf[h, group].reshape(PLANE * rows, HD)
            values = jnp.concatenate([values, jnp.ones((PLANE * rows, HD), bf)], axis=1)
            scores = lax.dot_general(qbuf[h, i], keys, (((1,), (1,)), ((), ())), preferred_element_type=f32)
            peak = jnp.broadcast_to(jnp.max(scores, axis=1, keepdims=True) * SHARP, (rows, HD))
            if not opening:
                old = top[h, i]
                peak = jnp.maximum(old, peak)
                fade = jnp.exp2(old - peak)
            weights = [
                jnp.exp2(scores[:, c : c + HD] * SHARP - peak).astype(bf) for c in range(0, PLANE * rows, HD)
            ]
            mixed = jnp.dot(jnp.concatenate(weights, axis=1), values, preferred_element_type=f32)
            if not opening:
                mixed = mixed + jnp.concatenate([fade, fade], axis=1) * summed[h, i]
            if closing:
                obuf[h, i] = (mixed[:, :HD] / mixed[:, HD:]).astype(bf)
            else:
                top[h, i] = peak
                summed[h, i] = mixed
            return carry

        lax.fori_loop(0, LINE, block_of, 0, unroll=True)
        if closing:
            for e in FAR:
                n = h * 3 + e - 1
                send(
                    obuf.at[h, lax.div(later(e), PLANE)], arecv.at[h, z],
                    os.at[n], orr.at[n], {"frame": later(e)}, late if h == last else sends,
                )
            arecv[h, z] = obuf[h, z]

    spot = lax.rem(f, PLANE)
    plane = ((to_x, spot + step_x), (to_y, spot + step_y), (to_xy, spot + step_x + step_y))

    def mod(stage):
        if stage == 0:
            loads[0].wait()
            t = te_ref[...]
            emb = t / (1.0 + jnp.exp(-t))
            high = emb.astype(bf).astype(f32)
            middle = (emb - high).astype(bf).astype(f32)
            low = emb - high - middle
            row = lax.broadcasted_iota(jnp.int32, (8, emb.shape[1]), 0)
            split = jnp.where(row == 0, high, jnp.where(row == 1, middle, jnp.where(row == 2, low, 0.0)))
            split = split.astype(bf)
            for c in range(3):
                for side in range(2):
                    term = jnp.dot(
                        split, tbuf[c, :, side * owned : (side + 1) * owned], preferred_element_type=f32
                    )
                    part[side, c : c + 1, :] = jnp.sum(term, axis=0, keepdims=True)
            send(part.at[1 - hd], mpart, ms.at[0], mr.at[0], to_pair)
            for h in range(heads):
                for j in range(LINE):
                    block, at = weight(h, j, 1 - hd)
                    n = h * LINE + j
                    send(block, wother.at[h, at], ws.at[n], wr.at[n], to_pair)
        elif stage == 1:
            remote(part.at[1 - hd], mpart, ms.at[0], mr.at[0], to_pair).wait_recv()
            macc[...] = part[hd] + mpart[...]
            for i, (peer, theirs) in enumerate(plane):
                send(quarter_of(macc, theirs), mrs.at[i + 1], ms.at[1 + i], mr.at[1 + i], peer)
            keep = pltpu.make_async_copy(quarter_of(macc, spot), mrs.at[0], own_sem.at[3 * heads])
            keep.start()
            keep.wait()
        elif stage == 2:
            for i, (peer, theirs) in enumerate(plane):
                remote(mrs.at[i + 1], mrs.at[i + 1], ms.at[1 + i], mr.at[1 + i], peer).wait_recv()
            mz[0] = (mrs[0] + mrs[1]) + (mrs[2] + mrs[3])
            for d in range(1, LINE):
                send(mz.at[0], mz.at[d], ms.at[3 + d], mr.at[3 + d], {"frame": later(d)})
        elif stage == 3:
            for d in range(1, LINE):
                remote(mz.at[0], mz.at[d], ms.at[3 + d], mr.at[3 + d], {"frame": earlier(d)}).wait_recv()
            mz[LINE] = (mz[0] + mz[2]) + (mz[1] + mz[3])
            mine = quarter_of(mfin, spot)
            for i, (peer, theirs) in enumerate(plane):
                send(mz.at[LINE], mine, ms.at[7 + i], mr.at[7 + i], peer)
            keep = pltpu.make_async_copy(mz.at[LINE], mine, own_sem.at[3 * heads])
            keep.start()
            keep.wait()
        else:
            for i, (peer, theirs) in enumerate(plane):
                block = quarter_of(mfin, theirs)
                remote(block, block, ms.at[7 + i], mr.at[7 + i], peer).wait_recv()
            mfin[...] = mfin[...] + table_ref[...]

    def gathered(h):
        for d in range(1, LINE):
            n = h * 3 + d - 1
            block = arecv.at[h, lax.div(earlier(d), PLANE)]
            remote(block, block, os.at[n], orr.at[n], {"frame": earlier(d)}).wait_recv()
        for copy in loads[2 + h * LINE : 2 + (h + 1) * LINE]:
            copy.wait()
        return jnp.concatenate([arecv[h, j] for j in range(LINE)], axis=1)

    fresh = [True]
    tiles = [slice(at, at + TILE) for at in range(0, owned, TILE)]

    def project(h):
        attn = gathered(h)
        send(arecv.at[h], aother.at[h], fs.at[h], fr.at[h], to_pair)
        for at in tiles:
            share = jnp.dot(attn, wown[h, :, at], preferred_element_type=f32)
            pacc[:, at] = share if fresh[0] else pacc[:, at] + share
        fresh[0] = False
        for j in range(LINE):
            n = h * LINE + j
            block, at = weight(h, j, hd)
            remote(block, wother.at[h, pl.ds(j * HD, HD)], ws.at[n], wr.at[n], to_pair).wait_recv()

    def partner(h):
        remote(arecv.at[h], aother.at[h], fs.at[h], fr.at[h], to_pair).wait_recv()
        return jnp.concatenate([aother[h, j] for j in range(LINE)], axis=1)

    def merge(h):
        attn = partner(h)
        for at in tiles:
            pacc[:, at] = pacc[:, at] + jnp.dot(attn, wother[h, :, at], preferred_element_type=f32)

    done = [0] * heads
    todo = {
        "launch": launch, "query": query, "first": first, "second_x": second_x, "second_y": second_y,
        "absorb": absorb, "mod": mod, "project": project, "merge": merge,
    }
    for name, *of in plan:
        if name not in ("project", "merge") or of[0] != last:
            todo[name](*of)
    mod(4)
    outs = [pltpu.make_async_copy(mfin, mod_hbm, out_sem.at[owned // TILE])]
    outs[0].start()
    loads[1].wait()
    for copy in sends:
        copy.wait_send()
    sends.clear()
    project(last)
    attn = partner(last)
    sum_lanes = jnp.zeros((rows, 128), f32)
    square_lanes = jnp.zeros((rows, 128), f32)
    for i in range(owned // TILE):
        at = slice(i * TILE, (i + 1) * TILE)
        mine = pacc[:, at] + jnp.dot(attn, wother[last, :, at], preferred_element_type=f32)
        hidden = (rbuf[:, at].astype(f32) + mfin[0:1, at] * mine).astype(bf)
        hbuf[:, at] = hidden
        outs.append(pltpu.make_async_copy(hbuf.at[:, at], hidden_hbm.at[:, at], out_sem.at[i]))
        outs[-1].start()
        wide = hidden.astype(f32)
        for c in range(0, TILE, 128):
            lane = wide[:, c : c + 128]
            sum_lanes += lane
            square_lanes += lane * lane
    stat[0] = sum_lanes
    stat[1] = square_lanes
    send(stat, stat_in, ss.at[1], sr.at[1], to_pair)
    remote(stat, stat_in, ss.at[1], sr.at[1], to_pair).wait_recv()
    mean = jnp.sum(stat[0] + stat_in[0], axis=1, keepdims=True) / D
    var = jnp.sum(stat[1] + stat_in[1], axis=1, keepdims=True) / D - mean * mean
    row_ref[0] = jnp.broadcast_to(mean, (rows, 128))
    row_ref[1] = jnp.broadcast_to(lax.rsqrt(var + 1e-06), (rows, 128))
    for copy in outs:
        copy.wait()
    for copy in sends + late:
        copy.wait_send()


def finish_kernel(hidden_hbm, row_hbm, mod_hbm, hidden_out, mlp_out, hbuf, mbuf, row, mod, sem, in_sem, out_sem, mlp_sem):
    rows, owned = hbuf.shape
    step = rows // CHUNKS
    small = [pltpu.make_async_copy(row_hbm, row, sem.at[0]), pltpu.make_async_copy(mod_hbm, mod, sem.at[1])]
    parts = [pl.ds(i * step, step) for i in range(CHUNKS)]
    loads = [pltpu.make_async_copy(hidden_hbm.at[at], hbuf.at[at], in_sem.at[i]) for i, at in enumerate(parts)]
    for copy in small + loads:
        copy.start()
    for copy in small:
        copy.wait()
    outs = []
    for i, at in enumerate(parts):
        loads[i].wait()
        outs.append(pltpu.make_async_copy(hbuf.at[at], hidden_out.at[at], out_sem.at[i]))
        outs[-1].start()
        for c in range(0, owned, 128):
            lane = slice(c, c + 128)
            wide = hbuf[at, lane].astype(jnp.float32)
            mbuf[at, lane] = (
                (wide - row[0, at]) * row[1, at] * (1.0 + mod[2:3, lane]) + mod[1:2, lane]
            ).astype(jnp.bfloat16)
        outs.append(pltpu.make_async_copy(mbuf.at[at], mlp_out.at[at], mlp_sem.at[i]))
        outs[-1].start()
    for copy in outs:
        copy.wait()


def fused_block(
    residual, query_proj, key_proj, value_proj, q_gain, k_gain, time_embed, time_proj, mod_table, out_weight
):
    rows, cols = query_proj.shape
    width = cols // LINE
    heads = width // HD
    owned = residual.shape[1]
    half_mod = mod_table.shape
    quarter = (half_mod[0], owned // PLANE)
    bf, f32 = jnp.bfloat16, jnp.float32
    dma = pltpu.SemaphoreType.DMA
    vmem = pl.BlockSpec(memory_space=pltpu.VMEM)
    hbm = pl.BlockSpec(memory_space=pl.ANY)
    blocks = LINE * PLANE
    count = heads * LINE * 2
    lines = time_proj.transpose(1, 0, 2)
    out = jax.ShapeDtypeStruct((rows, owned), bf)
    flat = pltpu.VMEM((rows, cols), bf)
    slab = pltpu.VMEM((heads, LINE, rows, HD), bf)
    lanes = pltpu.VMEM((2, rows, 128), f32)
    hidden, row, mod = pl.pallas_call(
        block_kernel,
        out_shape=(out, jax.ShapeDtypeStruct((2, rows, 128), f32), jax.ShapeDtypeStruct(half_mod, f32)),
        in_specs=[hbm, hbm, hbm, vmem, vmem, vmem, vmem, hbm, hbm, hbm],
        out_specs=(hbm, vmem, hbm),
        scratch_shapes=[
            flat, flat, flat, flat,
            pltpu.VMEM((heads, blocks, rows, HD), bf),
            pltpu.VMEM((heads, blocks, rows, HD), bf),
            slab, slab, slab,
            pltpu.VMEM((heads, LINE, rows, HD), f32),
            pltpu.VMEM((heads, LINE, rows, 2 * HD), f32),
            lanes, lanes, lanes,
            pltpu.VMEM((2,) + half_mod, f32),
            pltpu.VMEM(half_mod, f32),
            pltpu.VMEM(half_mod, f32),
            pltpu.VMEM((PLANE,) + quarter, f32),
            pltpu.VMEM((LINE + 1,) + quarter, f32),
            pltpu.VMEM(half_mod, f32),
            pltpu.VMEM(lines.shape, bf),
            pltpu.VMEM((heads, LINE * HD, owned), bf),
            pltpu.VMEM((heads, LINE * HD, owned), bf),
            slab,
            pltpu.VMEM((rows, owned), bf),
            pltpu.VMEM((rows, owned), f32),
            pltpu.VMEM((rows, owned), bf),
            lanes, lanes,
            dma((owned // TILE + 1,)),
            dma((3 * heads + 1,)), dma((4 + heads * LINE,)), dma((9 * heads,)), dma((9 * heads,)),
        ]
        + [dma((count,))] * 8
        + [dma((3 * heads,))] * 2
        + [dma((10,))] * 2
        + [dma((heads * LINE,))] * 2
        + [dma((heads,))] * 2
        + [dma((2,))] * 2,
        compiler_params=pltpu.CompilerParams(
            collective_id=0, has_side_effects=True, vmem_limit_bytes=60 * 1024 * 1024
        ),
    )(
        query_proj, key_proj, value_proj, q_gain, k_gain,
        time_embed.reshape(1, -1), mod_table, residual, lines, out_weight,
    )
    return pl.pallas_call(
        finish_kernel,
        out_shape=(out, out),
        in_specs=[hbm, hbm, hbm],
        out_specs=(hbm, hbm),
        scratch_shapes=[
            pltpu.VMEM((rows, owned), bf),
            pltpu.VMEM((rows, owned), bf),
            pltpu.VMEM((2, rows, 128), f32),
            pltpu.VMEM(half_mod, f32),
            dma((2,)), dma((CHUNKS,)), dma((CHUNKS,)), dma((CHUNKS,)),
        ],
        compiler_params=pltpu.CompilerParams(vmem_limit_bytes=60 * 1024 * 1024),
    )(hidden, row, mod)


def accumulate(carry, queries, keys_block, values_block):
    count = keys_block.shape[0]
    heads_here = queries.shape[1]
    keys_three = keys_block.reshape(count, heads_here, HD)
    values_three = values_block.reshape(count, heads_here, HD).astype(jnp.float32)
    scores = jnp.einsum("thd,shd->ths", queries, keys_three, preferred_element_type=jnp.float32) * (
        1.0 / math.sqrt(HD)
    )
    top_old, total_old, summed = carry
    top_new = jnp.maximum(top_old, jnp.max(scores, axis=2))
    weights = jnp.exp(scores - top_new[:, :, None])
    total_new = jnp.sum(weights, axis=2)
    summed_new = jnp.einsum("ths,shd->thd", weights, values_three, precision=lax.Precision.HIGHEST)
    return (top_new, total_new, summed_new)


def shards(
    residual,
    query_proj,
    key_proj,
    value_proj,
    q_gain,
    k_gain,
    time_embed,
    time_proj,
    mod_table,
    out_weight,
):
    if (
        lax.axis_size("head") == 2
        and lax.axis_size("frame") == LINE * PLANE
        and query_proj.shape[1] % (LINE * HD) == 0
    ):
        return fused_block(
            residual, query_proj, key_proj, value_proj, q_gain, k_gain, time_embed, time_proj, mod_table, out_weight
        )
    emb = jax.nn.silu(time_embed)
    partial_mod = jnp.einsum(
        "r,rcd->cd", emb, time_proj.astype(jnp.float32), precision=lax.Precision.HIGHEST
    )
    width = mod_table.shape[1]
    summed_mod = lax.psum(partial_mod, ("frame", "head"))
    share = lax.dynamic_slice_in_dim(summed_mod, lax.axis_index("head") * width, width, 1)
    modulation = mod_table + share
    gate = modulation[0]
    shift = modulation[1]
    scale = modulation[2]
    tok_rows = query_proj.shape[0]
    heads_here = query_proj.shape[1] // HD
    query_wide = query_proj.astype(jnp.float32)
    key_wide = key_proj.astype(jnp.float32)
    total_q, total_k = lax.psum(
        (jnp.sum(query_wide * query_wide, axis=1), jnp.sum(key_wide * key_wide, axis=1)), "head"
    )
    query_rms = lax.rsqrt(total_q / (HEADS * HD) + 1e-06)
    key_rms = lax.rsqrt(total_k / (HEADS * HD) + 1e-06)
    queries = (
        (query_wide * query_rms[:, None] * q_gain)
        .astype(jnp.bfloat16)
        .reshape(tok_rows, heads_here, HD)
    )
    start_state = (
        jnp.full((tok_rows, heads_here), -1e30, jnp.float32),
        jnp.zeros((tok_rows, heads_here), jnp.float32),
        jnp.zeros((tok_rows, heads_here, HD), jnp.float32),
    )
    every_scale = lax.all_gather(key_rms, "frame", axis=0, tiled=True)
    keys_block = (
        lax.all_gather(key_proj, "frame", axis=0, tiled=True).astype(jnp.float32)
        * every_scale[:, None]
        * k_gain
    ).astype(jnp.bfloat16)
    top_final, total_final, summed_final = accumulate(
        start_state, queries, keys_block, lax.all_gather(value_proj, "frame", axis=0, tiled=True)
    )
    attn = (
        (summed_final / total_final[:, :, None])
        .astype(jnp.bfloat16)
        .reshape(tok_rows, heads_here * HD)
    )
    proj = (
        lax.psum_scatter(
            lax.dot_general(
                out_weight, attn, (((0,), (1,)), ((), ())), preferred_element_type=jnp.float32
            ).astype(jnp.bfloat16),
            "head",
            scatter_dimension=0,
            tiled=True,
        )
        .astype(jnp.float32)
        .T
    )
    hidden_out = (residual.astype(jnp.float32) + gate * proj).astype(jnp.bfloat16)
    hidden32 = lax.optimization_barrier(hidden_out).astype(jnp.float32)
    row_sum, row_squares = lax.psum(
        (jnp.sum(hidden32, axis=1), jnp.sum(hidden32 * hidden32, axis=1)), "head"
    )
    mean = row_sum[:, None] / D
    var = row_squares[:, None] / D - mean * mean
    mlp_input = ((hidden32 - mean) * lax.rsqrt(var + 1e-06) * (1.0 + scale) + shift).astype(
        jnp.bfloat16
    )
    return (hidden_out, mlp_input)


def solution(mesh):
    in_specs = (
        P("frame", "head"),
        P("frame", "head"),
        P("frame", "head"),
        P("frame", "head"),
        P("head"),
        P("head"),
        P(("frame", "head")),
        P(("frame", "head"), None, None),
        P(None, "head"),
        P("head", None),
    )
    out_specs = (P("frame", "head"), P("frame", "head"))
    return jax.shard_map(shards, mesh=mesh, in_specs=in_specs, out_specs=out_specs, check_vma=False)
```

```python
import math

import jax
import jax.numpy as jnp
from jax import lax
from jax.experimental import pallas as pl
from jax.experimental.pallas import tpu as pltpu
from jax.sharding import PartitionSpec as P

D = 5120
HEADS = 24
HD = 128
SHARP = math.log2(math.e) / math.sqrt(HD)


MESH = pl.DeviceIdType.MESH
PLANE = 4
LINE = 4
TILE = 512
FAR = (1, 3, 2)
KEY, VALUE, QUERY = 0, 1, 2
ORDER = (
    (VALUE, 0), (VALUE, 1), (KEY, 0), (QUERY, 0), (KEY, 1), (VALUE, 2), (KEY, 2), (QUERY, 1), (QUERY, 2),
)
WINDOW = 4
CHUNKS = 2
BEAT = 2.9
UNIT = 0.72
HOP = 2.5
HOP_Z = 2.5
ABSORB = 0.4
PROJECT = 0.5


def remote(src, dst, send, recv, device):
    return pltpu.make_async_remote_copy(
        src_ref=src, dst_ref=dst, send_sem=send, recv_sem=recv, device_id=device, device_id_type=MESH
    )


def queue_of(heads):
    if heads == 3:
        return list(ORDER)
    return [(b, h) for h in range(heads) for b in (VALUE, KEY, QUERY)]


def agenda(heads):
    queue = queue_of(heads)
    free = {"x": 0.0, "y": 0.0, "z": 0.0}
    soon, waiting, steps = [], {}, []

    def travel(link, now, size):
        free[link] = max(free[link], now) + size
        return free[link]

    def after(key, count, at, step):
        left, late = waiting.get(key, (count, 0.0))
        waiting[key] = (left - 1, max(late, at))
        if left == 1:
            soon.append((max(late, at), len(steps) + len(soon), step))

    def arrived(at, d, h, b):
        for link, name in (("x", "second_x"), ("y", "second_y")):
            soon.append((travel(link, at, UNIT) + HOP, 0, (name, d, h, b)))

    def run(now, step):
        name, of = step[0], step[1:]
        if name == "launch":
            b, h = of
            for d in FAR:
                at = travel("z", now, BEAT / 3) + HOP_Z
                soon.append((at, 0, ("query", d, h) if b == QUERY else ("first", d, h, b)))
            if b != QUERY:
                arrived(now, 0, h, b)
        elif name == "first":
            arrived(now, *of)
            landed(now, of[2], of[1])
        elif name == "query":
            d, h = of
            for e in (0,) + FAR:
                after(("absorb", e, h), 7, now, ("absorb", e, h))
            landed(now, QUERY, h)
        elif name in ("second_x", "second_y"):
            d, h, b = of
            at = travel("y" if name == "second_x" else "x", now, UNIT / 2) + HOP
            after(("absorb", d, h), 7, at, ("absorb", d, h))
        elif name == "absorb":
            d, h = of
            after(("last", h), LINE, now, ("flush", h))
        elif name == "flush":
            (h,) = of
            for d in FAR:
                at = travel("z", now, BEAT / 3) + HOP_Z
                after(("project", h), 3, at, ("project", h))
        elif name == "project":
            soon.append((now + HOP, 0, ("merge",) + of))
        elif name == "mod" and of[0] < 3:
            soon.append((now + (HOP + 0.5, HOP + 0.5, HOP_Z + 0.5)[of[0]] + (free["z"] - now if of[0] == 2 else 0.0), 0, ("mod", of[0] + 1)))

    def landed(now, b, h):
        n = queue.index((b, h)) + WINDOW
        if n < len(queue):
            after(("launch", n), 3, now, ("launch",) + queue[n])

    now = 0.0
    soon.append((5.0, 0, ("mod", 0)))
    for n, pair in enumerate(queue[:WINDOW]):
        soon.append((0.0 if n == 0 else 2.5, -1, ("launch",) + pair))
    cost = {"absorb": ABSORB, "project": PROJECT, "merge": PROJECT, "mod": 0.6, "launch": 0.2}
    while soon:
        soon.sort(key=lambda entry: (entry[0], entry[1]))
        ready = [entry for entry in soon if entry[0] <= now + 0.02]
        light = [entry for entry in ready if entry[2][0] not in ("absorb", "project", "merge", "mod")]
        work = [entry for entry in ready if entry[2][0] not in ("project", "merge")]
        pick = (light or work or ready or soon)[0]
        soon.remove(pick)
        now = max(now, pick[0]) + cost.get(pick[2][0], 0.04)
        run(now, pick[2])
        steps.append((now, pick[2]))
    return [step for now, step in steps if step[0] != "flush"][WINDOW:]


def block_kernel(
    q_hbm, k_hbm, v_hbm, qg_ref, kg_ref, te_ref, table_ref, res_hbm, proj_hbm, weight_hbm,
    hidden_hbm, row_ref, mod_hbm,
    qraw, kraw, qn, kn, kbuf, vbuf, qbuf, obuf, arecv, top, summed,
    squares, squares_in, rms, part, mpart, macc, mrs, mz, mfin, tbuf, wown, wother, aother, rbuf, pacc, hbuf, stat, stat_in,
    out_sem,    own_sem, load_sem, zs, zr, xs, xr, ys, yr, dxs, dxr, dys, dyr, os, orr, ms, mr, ws, wr, fs, fr, ss, sr,
):
    f32, bf = jnp.float32, jnp.bfloat16
    frames = LINE * PLANE
    f = lax.axis_index("frame")
    hd = lax.axis_index("head")
    z = lax.div(f, PLANE)
    x = lax.rem(f, 2)
    y = lax.rem(lax.div(f, 2), 2)
    step_x = 1 - 2 * x
    step_y = 2 - 4 * y
    to_x = {"frame": f + step_x}
    to_y = {"frame": f + step_y}
    to_xy = {"frame": f + step_x + step_y}
    to_pair = {"head": 1 - hd}
    rows, cols_all = qn.shape
    half = rows // 2
    width = cols_all // LINE
    heads = width // HD
    owned = hbuf.shape[1]
    quarter = owned // PLANE

    def later(d):
        return lax.rem(f + PLANE * d, frames)

    def earlier(d):
        return lax.rem(f + frames - PLANE * d, frames)

    def piece(ref, line, h):
        return ref.at[:, pl.ds(pl.multiple_of(line * width + h * HD, HD), HD)]

    def quarter_of(ref, spot):
        return ref.at[:, pl.ds(pl.multiple_of(spot * quarter, 128), quarter)]

    sends, late = [], []
    plan = agenda(heads)
    last = plan[-1][1]

    def send(src, dst, s, r, peer, among=sends):
        copy = remote(src, dst, s, r, peer)
        copy.start()
        among.append(copy)

    barrier = pltpu.get_barrier_semaphore()
    for d in range(1, LINE):
        pl.semaphore_signal(barrier, inc=1, device_id={"frame": later(d)}, device_id_type=MESH)
    for peer in (to_x, to_y, to_xy, to_pair):
        pl.semaphore_signal(barrier, inc=1, device_id=peer, device_id_type=MESH)

    raw = []
    for i, (src, dst) in enumerate(((q_hbm, qraw), (k_hbm, kraw))):
        raw.append(pltpu.make_async_copy(src, dst, load_sem.at[i]))
        raw[i].start()
    loads = [pltpu.make_async_copy(proj_hbm, tbuf, load_sem.at[2])]
    loads.append(pltpu.make_async_copy(res_hbm, rbuf, load_sem.at[3]))
    def weight(h, j, side):
        columns = pl.ds(pl.multiple_of(side * owned, 128), owned)
        return weight_hbm.at[pl.ds(j * width + h * HD, HD), columns], pl.ds(j * HD, HD)

    for h in range(heads):
        for j in range(LINE):
            block, at = weight(h, j, hd)
            loads.append(pltpu.make_async_copy(block, wown.at[h, at], load_sem.at[4 + h * LINE + j]))
    for i, ref in enumerate((qraw, kraw)):
        raw[i].wait()
        lanes = jnp.zeros((rows, 128), f32)
        for c in range(0, cols_all, 128):
            wide = ref[:, c : c + 128].astype(f32)
            lanes += wide * wide
        squares[i] = lanes
    pl.semaphore_wait(barrier, LINE + 3)

    bufs = (kbuf, vbuf)
    own = {}

    def number(h, d, b):
        return (h * LINE + d) * 2 + b

    def send_line(b, h, src, dst):
        for d in FAR:
            peer = later(d)
            n = (b * heads + h) * 3 + d - 1
            send(piece(src, lax.div(peer, PLANE), h), dst, zs.at[n], zr.at[n], {"frame": peer})

    def send_own(b, h, src, dst):
        mine = piece(src, z, h)
        if b != QUERY:
            n = number(h, 0, b)
            send(mine, dst, xs.at[n], xr.at[n], to_x)
            send(mine, dst, ys.at[n], yr.at[n], to_y)
        own[b, h] = pltpu.make_async_copy(mine, dst, own_sem.at[b * heads + h])
        own[b, h].start()

    def launch(b, h):
        if b == VALUE:
            src, dst = v_hbm, vbuf.at[h, f]
        else:
            i, ref, gain, src, dst = (
                (1, kraw, kg_ref, kn, kbuf.at[h, f]) if b == KEY else (0, qraw, qg_ref, qn, qbuf.at[h, z])
            )
            for j in range(LINE):
                at = slice(j * width + h * HD, j * width + (h + 1) * HD)
                src[:, at] = (ref[:, at].astype(f32) * rms[i, :, 0:1] * gain[at].reshape(1, HD)).astype(bf)
        send_line(b, h, src, dst)
        send_own(b, h, src, dst)

    send(squares, squares_in, ss.at[0], sr.at[0], to_pair)
    launch(*queue_of(heads)[0])
    for copy in loads:
        copy.start()

    remote(squares, squares_in, ss.at[0], sr.at[0], to_pair).wait_recv()
    for i in range(2):
        sums = jnp.sum(squares[i] + squares_in[i], axis=1, keepdims=True)
        rms[i] = jnp.broadcast_to(lax.rsqrt(sums / (HEADS * HD) + 1e-06), (rows, 128))
    for b, h in queue_of(heads)[1:WINDOW]:
        launch(b, h)

    def first(d, h, b):
        n = number(h, d, b)
        m = (b * heads + h) * 3 + d - 1
        at = earlier(d)
        block = bufs[b].at[h, at]
        remote(block, block, zs.at[m], zr.at[m], {"frame": at}).wait_recv()
        send(block, block, xs.at[n], xr.at[n], to_x)
        send(block, block, ys.at[n], yr.at[n], to_y)

    def second_x(d, h, b):
        n = number(h, d, b)
        block = bufs[b].at[h, earlier(d) + step_x]
        remote(block, block, xs.at[n], xr.at[n], to_x).wait_recv()
        low = block.at[pl.ds(half, half)]
        send(low, low, dys.at[n], dyr.at[n], to_y)

    def second_y(d, h, b):
        n = number(h, d, b)
        block = bufs[b].at[h, earlier(d) + step_y]
        remote(block, block, ys.at[n], yr.at[n], to_y).wait_recv()
        high = block.at[pl.ds(0, half)]
        send(high, high, dxs.at[n], dxr.at[n], to_x)

    def third(d, h, b):
        n = number(h, d, b)
        block = bufs[b].at[h, earlier(d) + step_x + step_y]
        high = block.at[pl.ds(0, half)]
        remote(high, high, dxs.at[n], dxr.at[n], to_x).wait_recv()
        low = block.at[pl.ds(half, half)]
        remote(low, low, dys.at[n], dyr.at[n], to_y).wait_recv()

    def query(d, h):
        m = (QUERY * heads + h) * 3 + d - 1
        block = qbuf.at[h, lax.div(earlier(d), PLANE)]
        remote(block, block, zs.at[m], zr.at[m], {"frame": earlier(d)}).wait_recv()

    def absorb(d, h):
        opening, closing = done[h] == 0, done[h] == LINE - 1
        done[h] += 1
        if d == 0:
            own[KEY, h].wait()
            own[VALUE, h].wait()
        if opening:
            own[QUERY, h].wait()
        third(d, h, KEY)
        third(d, h, VALUE)
        base = pl.multiple_of(lax.div(earlier(d), PLANE) * PLANE, PLANE)
        group = pl.ds(base, PLANE)

        def block_of(i, carry):
            keys = kbuf[h, group].reshape(PLANE * rows, HD)
            values = vbuf[h, group].reshape(PLANE * rows, HD)
            values = jnp.concatenate([values, jnp.ones((PLANE * rows, HD), bf)], axis=1)
            scores = lax.dot_general(qbuf[h, i], keys, (((1,), (1,)), ((), ())), preferred_element_type=f32)
            peak = jnp.broadcast_to(jnp.max(scores, axis=1, keepdims=True) * SHARP, (rows, HD))
            if not opening:
                old = top[h, i]
                peak = jnp.maximum(old, peak)
                fade = jnp.exp2(old - peak)
            weights = [
                jnp.exp2(scores[:, c : c + HD] * SHARP - peak).astype(bf) for c in range(0, PLANE * rows, HD)
            ]
            mixed = jnp.dot(jnp.concatenate(weights, axis=1), values, preferred_element_type=f32)
            if not opening:
                mixed = mixed + jnp.concatenate([fade, fade], axis=1) * summed[h, i]
            if closing:
                obuf[h, i] = (mixed[:, :HD] / mixed[:, HD:]).astype(bf)
            else:
                top[h, i] = peak
                summed[h, i] = mixed
            return carry

        lax.fori_loop(0, LINE, block_of, 0, unroll=True)
        if closing:
            for e in FAR:
                n = h * 3 + e - 1
                send(
                    obuf.at[h, lax.div(later(e), PLANE)], arecv.at[h, z],
                    os.at[n], orr.at[n], {"frame": later(e)}, late if h == last else sends,
                )
            arecv[h, z] = obuf[h, z]

    spot = lax.rem(f, PLANE)
    plane = ((to_x, spot + step_x), (to_y, spot + step_y), (to_xy, spot + step_x + step_y))

    def mod(stage):
        if stage == 0:
            loads[0].wait()
            t = te_ref[...]
            emb = t / (1.0 + jnp.exp(-t))
            high = emb.astype(bf).astype(f32)
            middle = (emb - high).astype(bf).astype(f32)
            low = emb - high - middle
            row = lax.broadcasted_iota(jnp.int32, (8, emb.shape[1]), 0)
            split = jnp.where(row == 0, high, jnp.where(row == 1, middle, jnp.where(row == 2, low, 0.0)))
            split = split.astype(bf)
            for c in range(3):
                for side in range(2):
                    term = jnp.dot(
                        split, tbuf[c, :, side * owned : (side + 1) * owned], preferred_element_type=f32
                    )
                    part[side, c : c + 1, :] = jnp.sum(term, axis=0, keepdims=True)
            send(part.at[1 - hd], mpart, ms.at[0], mr.at[0], to_pair)
            for h in range(heads):
                for j in range(LINE):
                    block, at = weight(h, j, 1 - hd)
                    n = h * LINE + j
                    send(block, wother.at[h, at], ws.at[n], wr.at[n], to_pair)
        elif stage == 1:
            remote(part.at[1 - hd], mpart, ms.at[0], mr.at[0], to_pair).wait_recv()
            macc[...] = part[hd] + mpart[...]
            for i, (peer, theirs) in enumerate(plane):
                send(quarter_of(macc, theirs), mrs.at[i + 1], ms.at[1 + i], mr.at[1 + i], peer)
            keep = pltpu.make_async_copy(quarter_of(macc, spot), mrs.at[0], own_sem.at[3 * heads])
            keep.start()
            keep.wait()
        elif stage == 2:
            for i, (peer, theirs) in enumerate(plane):
                remote(mrs.at[i + 1], mrs.at[i + 1], ms.at[1 + i], mr.at[1 + i], peer).wait_recv()
            mz[0] = (mrs[0] + mrs[1]) + (mrs[2] + mrs[3])
            for d in range(1, LINE):
                send(mz.at[0], mz.at[d], ms.at[3 + d], mr.at[3 + d], {"frame": later(d)})
        elif stage == 3:
            for d in range(1, LINE):
                remote(mz.at[0], mz.at[d], ms.at[3 + d], mr.at[3 + d], {"frame": earlier(d)}).wait_recv()
            mz[LINE] = (mz[0] + mz[2]) + (mz[1] + mz[3])
            mine = quarter_of(mfin, spot)
            for i, (peer, theirs) in enumerate(plane):
                send(mz.at[LINE], mine, ms.at[7 + i], mr.at[7 + i], peer)
            keep = pltpu.make_async_copy(mz.at[LINE], mine, own_sem.at[3 * heads])
            keep.start()
            keep.wait()
        else:
            for i, (peer, theirs) in enumerate(plane):
                block = quarter_of(mfin, theirs)
                remote(block, block, ms.at[7 + i], mr.at[7 + i], peer).wait_recv()
            mfin[...] = mfin[...] + table_ref[...]

    def gathered(h):
        for d in range(1, LINE):
            n = h * 3 + d - 1
            block = arecv.at[h, lax.div(earlier(d), PLANE)]
            remote(block, block, os.at[n], orr.at[n], {"frame": earlier(d)}).wait_recv()
        for copy in loads[2 + h * LINE : 2 + (h + 1) * LINE]:
            copy.wait()
        return jnp.concatenate([arecv[h, j] for j in range(LINE)], axis=1)

    fresh = [True]
    tiles = [slice(at, at + TILE) for at in range(0, owned, TILE)]

    def project(h):
        attn = gathered(h)
        send(arecv.at[h], aother.at[h], fs.at[h], fr.at[h], to_pair)
        for at in tiles:
            share = jnp.dot(attn, wown[h, :, at], preferred_element_type=f32)
            pacc[:, at] = share if fresh[0] else pacc[:, at] + share
        fresh[0] = False
        for j in range(LINE):
            n = h * LINE + j
            block, at = weight(h, j, hd)
            remote(block, wother.at[h, pl.ds(j * HD, HD)], ws.at[n], wr.at[n], to_pair).wait_recv()

    def partner(h):
        remote(arecv.at[h], aother.at[h], fs.at[h], fr.at[h], to_pair).wait_recv()
        return jnp.concatenate([aother[h, j] for j in range(LINE)], axis=1)

    def merge(h):
        attn = partner(h)
        for at in tiles:
            pacc[:, at] = pacc[:, at] + jnp.dot(attn, wother[h, :, at], preferred_element_type=f32)

    done = [0] * heads
    todo = {
        "launch": launch, "query": query, "first": first, "second_x": second_x, "second_y": second_y,
        "absorb": absorb, "mod": mod, "project": project, "merge": merge,
    }
    for name, *of in plan:
        if name not in ("project", "merge") or of[0] != last:
            todo[name](*of)
    mod(4)
    outs = [pltpu.make_async_copy(mfin, mod_hbm, out_sem.at[owned // TILE])]
    outs[0].start()
    loads[1].wait()
    for copy in sends:
        copy.wait_send()
    sends.clear()
    project(last)
    attn = partner(last)
    sum_lanes = jnp.zeros((rows, 128), f32)
    square_lanes = jnp.zeros((rows, 128), f32)
    for i in range(owned // TILE):
        at = slice(i * TILE, (i + 1) * TILE)
        mine = pacc[:, at] + jnp.dot(attn, wother[last, :, at], preferred_element_type=f32)
        hidden = (rbuf[:, at].astype(f32) + mfin[0:1, at] * mine).astype(bf)
        hbuf[:, at] = hidden
        outs.append(pltpu.make_async_copy(hbuf.at[:, at], hidden_hbm.at[:, at], out_sem.at[i]))
        outs[-1].start()
        wide = hidden.astype(f32)
        for c in range(0, TILE, 128):
            lane = wide[:, c : c + 128]
            sum_lanes += lane
            square_lanes += lane * lane
    stat[0] = sum_lanes
    stat[1] = square_lanes
    send(stat, stat_in, ss.at[1], sr.at[1], to_pair)
    remote(stat, stat_in, ss.at[1], sr.at[1], to_pair).wait_recv()
    mean = jnp.sum(stat[0] + stat_in[0], axis=1, keepdims=True) / D
    var = jnp.sum(stat[1] + stat_in[1], axis=1, keepdims=True) / D - mean * mean
    row_ref[0] = jnp.broadcast_to(mean, (rows, 128))
    row_ref[1] = jnp.broadcast_to(lax.rsqrt(var + 1e-06), (rows, 128))
    for copy in outs:
        copy.wait()
    for copy in sends + late:
        copy.wait_send()


def finish_kernel(hidden_hbm, row_hbm, mod_hbm, hidden_out, mlp_out, hbuf, mbuf, row, mod, sem, in_sem, out_sem, mlp_sem):
    rows, owned = hbuf.shape
    step = rows // CHUNKS
    small = [pltpu.make_async_copy(row_hbm, row, sem.at[0]), pltpu.make_async_copy(mod_hbm, mod, sem.at[1])]
    parts = [pl.ds(i * step, step) for i in range(CHUNKS)]
    loads = [pltpu.make_async_copy(hidden_hbm.at[at], hbuf.at[at], in_sem.at[i]) for i, at in enumerate(parts)]
    for copy in small + loads:
        copy.start()
    for copy in small:
        copy.wait()
    outs = []
    for i, at in enumerate(parts):
        loads[i].wait()
        outs.append(pltpu.make_async_copy(hbuf.at[at], hidden_out.at[at], out_sem.at[i]))
        outs[-1].start()
        for c in range(0, owned, 128):
            lane = slice(c, c + 128)
            wide = hbuf[at, lane].astype(jnp.float32)
            mbuf[at, lane] = (
                (wide - row[0, at]) * row[1, at] * (1.0 + mod[2:3, lane]) + mod[1:2, lane]
            ).astype(jnp.bfloat16)
        outs.append(pltpu.make_async_copy(mbuf.at[at], mlp_out.at[at], mlp_sem.at[i]))
        outs[-1].start()
    for copy in outs:
        copy.wait()


def fused_block(
    residual, query_proj, key_proj, value_proj, q_gain, k_gain, time_embed, time_proj, mod_table, out_weight
):
    rows, cols = query_proj.shape
    width = cols // LINE
    heads = width // HD
    owned = residual.shape[1]
    half_mod = mod_table.shape
    quarter = (half_mod[0], owned // PLANE)
    bf, f32 = jnp.bfloat16, jnp.float32
    dma = pltpu.SemaphoreType.DMA
    vmem = pl.BlockSpec(memory_space=pltpu.VMEM)
    hbm = pl.BlockSpec(memory_space=pl.ANY)
    blocks = LINE * PLANE
    count = heads * LINE * 2
    lines = time_proj.transpose(1, 0, 2)
    out = jax.ShapeDtypeStruct((rows, owned), bf)
    flat = pltpu.VMEM((rows, cols), bf)
    slab = pltpu.VMEM((heads, LINE, rows, HD), bf)
    lanes = pltpu.VMEM((2, rows, 128), f32)
    hidden, row, mod = pl.pallas_call(
        block_kernel,
        out_shape=(out, jax.ShapeDtypeStruct((2, rows, 128), f32), jax.ShapeDtypeStruct(half_mod, f32)),
        in_specs=[hbm, hbm, hbm, vmem, vmem, vmem, vmem, hbm, hbm, hbm],
        out_specs=(hbm, vmem, hbm),
        scratch_shapes=[
            flat, flat, flat, flat,
            pltpu.VMEM((heads, blocks, rows, HD), bf),
            pltpu.VMEM((heads, blocks, rows, HD), bf),
            slab, slab, slab,
            pltpu.VMEM((heads, LINE, rows, HD), f32),
            pltpu.VMEM((heads, LINE, rows, 2 * HD), f32),
            lanes, lanes, lanes,
            pltpu.VMEM((2,) + half_mod, f32),
            pltpu.VMEM(half_mod, f32),
            pltpu.VMEM(half_mod, f32),
            pltpu.VMEM((PLANE,) + quarter, f32),
            pltpu.VMEM((LINE + 1,) + quarter, f32),
            pltpu.VMEM(half_mod, f32),
            pltpu.VMEM(lines.shape, bf),
            pltpu.VMEM((heads, LINE * HD, owned), bf),
            pltpu.VMEM((heads, LINE * HD, owned), bf),
            slab,
            pltpu.VMEM((rows, owned), bf),
            pltpu.VMEM((rows, owned), f32),
            pltpu.VMEM((rows, owned), bf),
            lanes, lanes,
            dma((owned // TILE + 1,)),
            dma((3 * heads + 1,)), dma((4 + heads * LINE,)), dma((9 * heads,)), dma((9 * heads,)),
        ]
        + [dma((count,))] * 8
        + [dma((3 * heads,))] * 2
        + [dma((10,))] * 2
        + [dma((heads * LINE,))] * 2
        + [dma((heads,))] * 2
        + [dma((2,))] * 2,
        compiler_params=pltpu.CompilerParams(
            collective_id=0, has_side_effects=True, vmem_limit_bytes=60 * 1024 * 1024
        ),
    )(
        query_proj, key_proj, value_proj, q_gain, k_gain,
        time_embed.reshape(1, -1), mod_table, residual, lines, out_weight,
    )
    return pl.pallas_call(
        finish_kernel,
        out_shape=(out, out),
        in_specs=[hbm, hbm, hbm],
        out_specs=(hbm, hbm),
        scratch_shapes=[
            pltpu.VMEM((rows, owned), bf),
            pltpu.VMEM((rows, owned), bf),
            pltpu.VMEM((2, rows, 128), f32),
            pltpu.VMEM(half_mod, f32),
            dma((2,)), dma((CHUNKS,)), dma((CHUNKS,)), dma((CHUNKS,)),
        ],
        compiler_params=pltpu.CompilerParams(vmem_limit_bytes=60 * 1024 * 1024),
    )(hidden, row, mod)


def accumulate(carry, queries, keys_block, values_block):
    count = keys_block.shape[0]
    heads_here = queries.shape[1]
    keys_three = keys_block.reshape(count, heads_here, HD)
    values_three = values_block.reshape(count, heads_here, HD).astype(jnp.float32)
    scores = jnp.einsum("thd,shd->ths", queries, keys_three, preferred_element_type=jnp.float32) * (
        1.0 / math.sqrt(HD)
    )
    top_old, total_old, summed = carry
    top_new = jnp.maximum(top_old, jnp.max(scores, axis=2))
    weights = jnp.exp(scores - top_new[:, :, None])
    total_new = jnp.sum(weights, axis=2)
    summed_new = jnp.einsum("ths,shd->thd", weights, values_three, precision=lax.Precision.HIGHEST)
    return (top_new, total_new, summed_new)


def shards(
    residual,
    query_proj,
    key_proj,
    value_proj,
    q_gain,
    k_gain,
    time_embed,
    time_proj,
    mod_table,
    out_weight,
):
    if (
        lax.axis_size("head") == 2
        and lax.axis_size("frame") == LINE * PLANE
        and query_proj.shape[1] % (LINE * HD) == 0
    ):
        return fused_block(
            residual, query_proj, key_proj, value_proj, q_gain, k_gain, time_embed, time_proj, mod_table, out_weight
        )
    emb = jax.nn.silu(time_embed)
    partial_mod = jnp.einsum(
        "r,rcd->cd", emb, time_proj.astype(jnp.float32), precision=lax.Precision.HIGHEST
    )
    width = mod_table.shape[1]
    summed_mod = lax.psum(partial_mod, ("frame", "head"))
    share = lax.dynamic_slice_in_dim(summed_mod, lax.axis_index("head") * width, width, 1)
    modulation = mod_table + share
    gate = modulation[0]
    shift = modulation[1]
    scale = modulation[2]
    tok_rows = query_proj.shape[0]
    heads_here = query_proj.shape[1] // HD
    query_wide = query_proj.astype(jnp.float32)
    key_wide = key_proj.astype(jnp.float32)
    total_q, total_k = lax.psum(
        (jnp.sum(query_wide * query_wide, axis=1), jnp.sum(key_wide * key_wide, axis=1)), "head"
    )
    query_rms = lax.rsqrt(total_q / (HEADS * HD) + 1e-06)
    key_rms = lax.rsqrt(total_k / (HEADS * HD) + 1e-06)
    queries = (
        (query_wide * query_rms[:, None] * q_gain)
        .astype(jnp.bfloat16)
        .reshape(tok_rows, heads_here, HD)
    )
    start_state = (
        jnp.full((tok_rows, heads_here), -1e30, jnp.float32),
        jnp.zeros((tok_rows, heads_here), jnp.float32),
        jnp.zeros((tok_rows, heads_here, HD), jnp.float32),
    )
    every_scale = lax.all_gather(key_rms, "frame", axis=0, tiled=True)
    keys_block = (
        lax.all_gather(key_proj, "frame", axis=0, tiled=True).astype(jnp.float32)
        * every_scale[:, None]
        * k_gain
    ).astype(jnp.bfloat16)
    top_final, total_final, summed_final = accumulate(
        start_state, queries, keys_block, lax.all_gather(value_proj, "frame", axis=0, tiled=True)
    )
    attn = (
        (summed_final / total_final[:, :, None])
        .astype(jnp.bfloat16)
        .reshape(tok_rows, heads_here * HD)
    )
    proj = (
        lax.psum_scatter(
            lax.dot_general(
                out_weight, attn, (((0,), (1,)), ((), ())), preferred_element_type=jnp.float32
            ).astype(jnp.bfloat16),
            "head",
            scatter_dimension=0,
            tiled=True,
        )
        .astype(jnp.float32)
        .T
    )
    hidden_out = (residual.astype(jnp.float32) + gate * proj).astype(jnp.bfloat16)
    hidden32 = lax.optimization_barrier(hidden_out).astype(jnp.float32)
    row_sum, row_squares = lax.psum(
        (jnp.sum(hidden32, axis=1), jnp.sum(hidden32 * hidden32, axis=1)), "head"
    )
    mean = row_sum[:, None] / D
    var = row_squares[:, None] / D - mean * mean
    mlp_input = ((hidden32 - mean) * lax.rsqrt(var + 1e-06) * (1.0 + scale) + shift).astype(
        jnp.bfloat16
    )
    return (hidden_out, mlp_input)


def solution(mesh):
    in_specs = (
        P("frame", "head"),
        P("frame", "head"),
        P("frame", "head"),
        P("frame", "head"),
        P("head"),
        P("head"),
        P(("frame", "head")),
        P(("frame", "head"), None, None),
        P(None, "head"),
        P("head", None),
    )
    out_specs = (P("frame", "head"), P("frame", "head"))
    return jax.shard_map(shards, mesh=mesh, in_specs=in_specs, out_specs=out_specs, check_vma=False)
```

```python
import math

import jax
import jax.numpy as jnp
from jax import lax
from jax.experimental import pallas as pl
from jax.experimental.pallas import tpu as pltpu
from jax.sharding import PartitionSpec as P

D = 5120
HEADS = 24
HD = 128
SHARP = math.log2(math.e) / math.sqrt(HD)


MESH = pl.DeviceIdType.MESH
PLANE = 4
LINE = 4
TILE = 512
FAR = (1, 3, 2)
KEY, VALUE, QUERY = 0, 1, 2
ORDER = (
    (VALUE, 0), (VALUE, 1), (KEY, 0), (QUERY, 0), (KEY, 1), (VALUE, 2), (KEY, 2), (QUERY, 1), (QUERY, 2),
)
WINDOW = 4
CHUNKS = 2
BEAT = 2.9
UNIT = 0.72
HOP = 2.5
HOP_Z = 3.0
ABSORB = 0.4
PROJECT = 0.5


def remote(src, dst, send, recv, device):
    return pltpu.make_async_remote_copy(
        src_ref=src, dst_ref=dst, send_sem=send, recv_sem=recv, device_id=device, device_id_type=MESH
    )


def queue_of(heads):
    if heads == 3:
        return list(ORDER)
    return [(b, h) for h in range(heads) for b in (VALUE, KEY, QUERY)]


def agenda(heads):
    queue = queue_of(heads)
    free = {"x": 0.0, "y": 0.0, "z": 0.0}
    soon, waiting, steps = [], {}, []

    def travel(link, now, size):
        free[link] = max(free[link], now) + size
        return free[link]

    def after(key, count, at, step):
        left, late = waiting.get(key, (count, 0.0))
        waiting[key] = (left - 1, max(late, at))
        if left == 1:
            soon.append((max(late, at), len(steps) + len(soon), step))

    def arrived(at, d, h, b):
        for link, name in (("x", "second_x"), ("y", "second_y")):
            soon.append((travel(link, at, UNIT) + HOP, 0, (name, d, h, b)))

    def run(now, step):
        name, of = step[0], step[1:]
        if name == "launch":
            b, h = of
            for d in FAR:
                at = travel("z", now, BEAT / 3) + HOP_Z
                soon.append((at, 0, ("query", d, h) if b == QUERY else ("first", d, h, b)))
            if b != QUERY:
                arrived(now, 0, h, b)
        elif name == "first":
            arrived(now, *of)
            landed(now, of[2], of[1])
        elif name == "query":
            d, h = of
            for e in (0,) + FAR:
                after(("absorb", e, h), 7, now, ("absorb", e, h))
            landed(now, QUERY, h)
        elif name in ("second_x", "second_y"):
            d, h, b = of
            at = travel("y" if name == "second_x" else "x", now, UNIT / 2) + HOP
            after(("absorb", d, h), 7, at, ("absorb", d, h))
        elif name == "absorb":
            d, h = of
            after(("last", h), LINE, now, ("flush", h))
        elif name == "flush":
            (h,) = of
            for d in FAR:
                at = travel("z", now, BEAT / 3) + HOP_Z
                after(("project", h), 3, at, ("project", h))
        elif name == "project":
            soon.append((now + HOP, 0, ("merge",) + of))
        elif name == "mod" and of[0] < 3:
            soon.append((now + (HOP + 0.5, HOP + 0.5, HOP_Z + 0.5)[of[0]] + (free["z"] - now if of[0] == 2 else 0.0), 0, ("mod", of[0] + 1)))

    def landed(now, b, h):
        n = queue.index((b, h)) + WINDOW
        if n < len(queue):
            after(("launch", n), 3, now, ("launch",) + queue[n])

    now = 0.0
    soon.append((5.0, 0, ("mod", 0)))
    for n, pair in enumerate(queue[:WINDOW]):
        soon.append((0.0 if n == 0 else 2.5, -1, ("launch",) + pair))
    cost = {"absorb": ABSORB, "project": PROJECT, "merge": PROJECT, "mod": 0.6, "launch": 0.2}
    while soon:
        soon.sort(key=lambda entry: (entry[0], entry[1]))
        ready = [entry for entry in soon if entry[0] <= now + 0.02]
        light = [entry for entry in ready if entry[2][0] not in ("absorb", "project", "merge", "mod")]
        work = [entry for entry in ready if entry[2][0] not in ("project", "merge")]
        pick = (light or work or ready or soon)[0]
        soon.remove(pick)
        now = max(now, pick[0]) + cost.get(pick[2][0], 0.04)
        run(now, pick[2])
        steps.append((now, pick[2]))
    return [step for now, step in steps if step[0] != "flush"][WINDOW:]


def block_kernel(
    q_hbm, k_hbm, v_hbm, qg_ref, kg_ref, te_ref, table_ref, res_hbm, proj_hbm, weight_hbm,
    hidden_hbm, row_ref, mod_hbm,
    qraw, kraw, qn, kn, kbuf, vbuf, qbuf, obuf, arecv, top, summed,
    squares, squares_in, rms, part, mpart, macc, mrs, mz, mfin, tbuf, wown, wother, aother, rbuf, pacc, hbuf, stat, stat_in,
    out_sem,    own_sem, load_sem, zs, zr, xs, xr, ys, yr, dxs, dxr, dys, dyr, os, orr, ms, mr, ws, wr, fs, fr, ss, sr,
):
    f32, bf = jnp.float32, jnp.bfloat16
    frames = LINE * PLANE
    f = lax.axis_index("frame")
    hd = lax.axis_index("head")
    z = lax.div(f, PLANE)
    x = lax.rem(f, 2)
    y = lax.rem(lax.div(f, 2), 2)
    step_x = 1 - 2 * x
    step_y = 2 - 4 * y
    to_x = {"frame": f + step_x}
    to_y = {"frame": f + step_y}
    to_xy = {"frame": f + step_x + step_y}
    to_pair = {"head": 1 - hd}
    rows, cols_all = qn.shape
    half = rows // 2
    width = cols_all // LINE
    heads = width // HD
    owned = hbuf.shape[1]
    quarter = owned // PLANE

    def later(d):
        return lax.rem(f + PLANE * d, frames)

    def earlier(d):
        return lax.rem(f + frames - PLANE * d, frames)

    def piece(ref, line, h):
        return ref.at[:, pl.ds(pl.multiple_of(line * width + h * HD, HD), HD)]

    def quarter_of(ref, spot):
        return ref.at[:, pl.ds(pl.multiple_of(spot * quarter, 128), quarter)]

    sends, late = [], []
    plan = agenda(heads)
    last = plan[-1][1]

    def send(src, dst, s, r, peer, among=sends):
        copy = remote(src, dst, s, r, peer)
        copy.start()
        among.append(copy)

    barrier = pltpu.get_barrier_semaphore()
    for d in range(1, LINE):
        pl.semaphore_signal(barrier, inc=1, device_id={"frame": later(d)}, device_id_type=MESH)
    for peer in (to_x, to_y, to_xy, to_pair):
        pl.semaphore_signal(barrier, inc=1, device_id=peer, device_id_type=MESH)

    raw = []
    for i, (src, dst) in enumerate(((q_hbm, qraw), (k_hbm, kraw))):
        raw.append(pltpu.make_async_copy(src, dst, load_sem.at[i]))
        raw[i].start()
    loads = [pltpu.make_async_copy(proj_hbm, tbuf, load_sem.at[2])]
    loads.append(pltpu.make_async_copy(res_hbm, rbuf, load_sem.at[3]))
    def weight(h, j, side):
        columns = pl.ds(pl.multiple_of(side * owned, 128), owned)
        return weight_hbm.at[pl.ds(j * width + h * HD, HD), columns], pl.ds(j * HD, HD)

    for h in range(heads):
        for j in range(LINE):
            block, at = weight(h, j, hd)
            loads.append(pltpu.make_async_copy(block, wown.at[h, at], load_sem.at[4 + h * LINE + j]))
    for i, ref in enumerate((qraw, kraw)):
        raw[i].wait()
        lanes = jnp.zeros((rows, 128), f32)
        for c in range(0, cols_all, 128):
            wide = ref[:, c : c + 128].astype(f32)
            lanes += wide * wide
        squares[i] = lanes
    pl.semaphore_wait(barrier, LINE + 3)

    bufs = (kbuf, vbuf)
    own = {}

    def number(h, d, b):
        return (h * LINE + d) * 2 + b

    def send_line(b, h, src, dst):
        for d in FAR:
            peer = later(d)
            n = (b * heads + h) * 3 + d - 1
            send(piece(src, lax.div(peer, PLANE), h), dst, zs.at[n], zr.at[n], {"frame": peer})

    def send_own(b, h, src, dst):
        mine = piece(src, z, h)
        if b != QUERY:
            n = number(h, 0, b)
            send(mine, dst, xs.at[n], xr.at[n], to_x)
            send(mine, dst, ys.at[n], yr.at[n], to_y)
        own[b, h] = pltpu.make_async_copy(mine, dst, own_sem.at[b * heads + h])
        own[b, h].start()

    def launch(b, h):
        if b == VALUE:
            src, dst = v_hbm, vbuf.at[h, f]
        else:
            i, ref, gain, src, dst = (
                (1, kraw, kg_ref, kn, kbuf.at[h, f]) if b == KEY else (0, qraw, qg_ref, qn, qbuf.at[h, z])
            )
            for j in range(LINE):
                at = slice(j * width + h * HD, j * width + (h + 1) * HD)
                src[:, at] = (ref[:, at].astype(f32) * rms[i, :, 0:1] * gain[at].reshape(1, HD)).astype(bf)
        send_line(b, h, src, dst)
        send_own(b, h, src, dst)

    send(squares, squares_in, ss.at[0], sr.at[0], to_pair)
    launch(*queue_of(heads)[0])
    for copy in loads:
        copy.start()

    remote(squares, squares_in, ss.at[0], sr.at[0], to_pair).wait_recv()
    for i in range(2):
        sums = jnp.sum(squares[i] + squares_in[i], axis=1, keepdims=True)
        rms[i] = jnp.broadcast_to(lax.rsqrt(sums / (HEADS * HD) + 1e-06), (rows, 128))
    for b, h in queue_of(heads)[1:WINDOW]:
        launch(b, h)

    def first(d, h, b):
        n = number(h, d, b)
        m = (b * heads + h) * 3 + d - 1
        at = earlier(d)
        block = bufs[b].at[h, at]
        remote(block, block, zs.at[m], zr.at[m], {"frame": at}).wait_recv()
        send(block, block, xs.at[n], xr.at[n], to_x)
        send(block, block, ys.at[n], yr.at[n], to_y)

    def second_x(d, h, b):
        n = number(h, d, b)
        block = bufs[b].at[h, earlier(d) + step_x]
        remote(block, block, xs.at[n], xr.at[n], to_x).wait_recv()
        low = block.at[pl.ds(half, half)]
        send(low, low, dys.at[n], dyr.at[n], to_y)

    def second_y(d, h, b):
        n = number(h, d, b)
        block = bufs[b].at[h, earlier(d) + step_y]
        remote(block, block, ys.at[n], yr.at[n], to_y).wait_recv()
        high = block.at[pl.ds(0, half)]
        send(high, high, dxs.at[n], dxr.at[n], to_x)

    def third(d, h, b):
        n = number(h, d, b)
        block = bufs[b].at[h, earlier(d) + step_x + step_y]
        high = block.at[pl.ds(0, half)]
        remote(high, high, dxs.at[n], dxr.at[n], to_x).wait_recv()
        low = block.at[pl.ds(half, half)]
        remote(low, low, dys.at[n], dyr.at[n], to_y).wait_recv()

    def query(d, h):
        m = (QUERY * heads + h) * 3 + d - 1
        block = qbuf.at[h, lax.div(earlier(d), PLANE)]
        remote(block, block, zs.at[m], zr.at[m], {"frame": earlier(d)}).wait_recv()

    def absorb(d, h):
        opening, closing = done[h] == 0, done[h] == LINE - 1
        done[h] += 1
        if d == 0:
            own[KEY, h].wait()
            own[VALUE, h].wait()
        if opening:
            own[QUERY, h].wait()
        third(d, h, KEY)
        third(d, h, VALUE)
        base = pl.multiple_of(lax.div(earlier(d), PLANE) * PLANE, PLANE)
        group = pl.ds(base, PLANE)

        def block_of(i, carry):
            keys = kbuf[h, group].reshape(PLANE * rows, HD)
            values = vbuf[h, group].reshape(PLANE * rows, HD)
            values = jnp.concatenate([values, jnp.ones((PLANE * rows, HD), bf)], axis=1)
            scores = lax.dot_general(qbuf[h, i], keys, (((1,), (1,)), ((), ())), preferred_element_type=f32)
            peak = jnp.broadcast_to(jnp.max(scores, axis=1, keepdims=True) * SHARP, (rows, HD))
            if not opening:
                old = top[h, i]
                peak = jnp.maximum(old, peak)
                fade = jnp.exp2(old - peak)
            weights = [
                jnp.exp2(scores[:, c : c + HD] * SHARP - peak).astype(bf) for c in range(0, PLANE * rows, HD)
            ]
            mixed = jnp.dot(jnp.concatenate(weights, axis=1), values, preferred_element_type=f32)
            if not opening:
                mixed = mixed + jnp.concatenate([fade, fade], axis=1) * summed[h, i]
            if closing:
                obuf[h, i] = (mixed[:, :HD] / mixed[:, HD:]).astype(bf)
            else:
                top[h, i] = peak
                summed[h, i] = mixed
            return carry

        lax.fori_loop(0, LINE, block_of, 0, unroll=True)
        if closing:
            for e in FAR:
                n = h * 3 + e - 1
                send(
                    obuf.at[h, lax.div(later(e), PLANE)], arecv.at[h, z],
                    os.at[n], orr.at[n], {"frame": later(e)}, late if h == last else sends,
                )
            arecv[h, z] = obuf[h, z]

    spot = lax.rem(f, PLANE)
    plane = ((to_x, spot + step_x), (to_y, spot + step_y), (to_xy, spot + step_x + step_y))

    def mod(stage):
        if stage == 0:
            loads[0].wait()
            t = te_ref[...]
            emb = t / (1.0 + jnp.exp(-t))
            high = emb.astype(bf).astype(f32)
            middle = (emb - high).astype(bf).astype(f32)
            low = emb - high - middle
            row = lax.broadcasted_iota(jnp.int32, (8, emb.shape[1]), 0)
            split = jnp.where(row == 0, high, jnp.where(row == 1, middle, jnp.where(row == 2, low, 0.0)))
            split = split.astype(bf)
            for c in range(3):
                for side in range(2):
                    term = jnp.dot(
                        split, tbuf[c, :, side * owned : (side + 1) * owned], preferred_element_type=f32
                    )
                    part[side, c : c + 1, :] = jnp.sum(term, axis=0, keepdims=True)
            send(part.at[1 - hd], mpart, ms.at[0], mr.at[0], to_pair)
            for h in range(heads):
                for j in range(LINE):
                    block, at = weight(h, j, 1 - hd)
                    n = h * LINE + j
                    send(block, wother.at[h, at], ws.at[n], wr.at[n], to_pair)
        elif stage == 1:
            remote(part.at[1 - hd], mpart, ms.at[0], mr.at[0], to_pair).wait_recv()
            macc[...] = part[hd] + mpart[...]
            for i, (peer, theirs) in enumerate(plane):
                send(quarter_of(macc, theirs), mrs.at[i + 1], ms.at[1 + i], mr.at[1 + i], peer)
            keep = pltpu.make_async_copy(quarter_of(macc, spot), mrs.at[0], own_sem.at[3 * heads])
            keep.start()
            keep.wait()
        elif stage == 2:
            for i, (peer, theirs) in enumerate(plane):
                remote(mrs.at[i + 1], mrs.at[i + 1], ms.at[1 + i], mr.at[1 + i], peer).wait_recv()
            mz[0] = (mrs[0] + mrs[1]) + (mrs[2] + mrs[3])
            for d in range(1, LINE):
                send(mz.at[0], mz.at[d], ms.at[3 + d], mr.at[3 + d], {"frame": later(d)})
        elif stage == 3:
            for d in range(1, LINE):
                remote(mz.at[0], mz.at[d], ms.at[3 + d], mr.at[3 + d], {"frame": earlier(d)}).wait_recv()
            mz[LINE] = (mz[0] + mz[2]) + (mz[1] + mz[3])
            mine = quarter_of(mfin, spot)
            for i, (peer, theirs) in enumerate(plane):
                send(mz.at[LINE], mine, ms.at[7 + i], mr.at[7 + i], peer)
            keep = pltpu.make_async_copy(mz.at[LINE], mine, own_sem.at[3 * heads])
            keep.start()
            keep.wait()
        else:
            for i, (peer, theirs) in enumerate(plane):
                block = quarter_of(mfin, theirs)
                remote(block, block, ms.at[7 + i], mr.at[7 + i], peer).wait_recv()
            mfin[...] = mfin[...] + table_ref[...]

    def gathered(h):
        for d in range(1, LINE):
            n = h * 3 + d - 1
            block = arecv.at[h, lax.div(earlier(d), PLANE)]
            remote(block, block, os.at[n], orr.at[n], {"frame": earlier(d)}).wait_recv()
        for copy in loads[2 + h * LINE : 2 + (h + 1) * LINE]:
            copy.wait()
        return jnp.concatenate([arecv[h, j] for j in range(LINE)], axis=1)

    fresh = [True]
    tiles = [slice(at, at + TILE) for at in range(0, owned, TILE)]

    def project(h):
        attn = gathered(h)
        send(arecv.at[h], aother.at[h], fs.at[h], fr.at[h], to_pair)
        for at in tiles:
            share = jnp.dot(attn, wown[h, :, at], preferred_element_type=f32)
            pacc[:, at] = share if fresh[0] else pacc[:, at] + share
        fresh[0] = False
        for j in range(LINE):
            n = h * LINE + j
            block, at = weight(h, j, hd)
            remote(block, wother.at[h, pl.ds(j * HD, HD)], ws.at[n], wr.at[n], to_pair).wait_recv()

    def partner(h):
        remote(arecv.at[h], aother.at[h], fs.at[h], fr.at[h], to_pair).wait_recv()
        return jnp.concatenate([aother[h, j] for j in range(LINE)], axis=1)

    def merge(h):
        attn = partner(h)
        for at in tiles:
            pacc[:, at] = pacc[:, at] + jnp.dot(attn, wother[h, :, at], preferred_element_type=f32)

    done = [0] * heads
    todo = {
        "launch": launch, "query": query, "first": first, "second_x": second_x, "second_y": second_y,
        "absorb": absorb, "mod": mod, "project": project, "merge": merge,
    }
    for name, *of in plan:
        if name not in ("project", "merge") or of[0] != last:
            todo[name](*of)
    mod(4)
    outs = [pltpu.make_async_copy(mfin, mod_hbm, out_sem.at[owned // TILE])]
    outs[0].start()
    loads[1].wait()
    for copy in sends:
        copy.wait_send()
    sends.clear()
    project(last)
    attn = partner(last)
    sum_lanes = jnp.zeros((rows, 128), f32)
    square_lanes = jnp.zeros((rows, 128), f32)
    for i in range(owned // TILE):
        at = slice(i * TILE, (i + 1) * TILE)
        mine = pacc[:, at] + jnp.dot(attn, wother[last, :, at], preferred_element_type=f32)
        hidden = (rbuf[:, at].astype(f32) + mfin[0:1, at] * mine).astype(bf)
        hbuf[:, at] = hidden
        outs.append(pltpu.make_async_copy(hbuf.at[:, at], hidden_hbm.at[:, at], out_sem.at[i]))
        outs[-1].start()
        wide = hidden.astype(f32)
        for c in range(0, TILE, 128):
            lane = wide[:, c : c + 128]
            sum_lanes += lane
            square_lanes += lane * lane
    stat[0] = sum_lanes
    stat[1] = square_lanes
    send(stat, stat_in, ss.at[1], sr.at[1], to_pair)
    remote(stat, stat_in, ss.at[1], sr.at[1], to_pair).wait_recv()
    mean = jnp.sum(stat[0] + stat_in[0], axis=1, keepdims=True) / D
    var = jnp.sum(stat[1] + stat_in[1], axis=1, keepdims=True) / D - mean * mean
    row_ref[0] = jnp.broadcast_to(mean, (rows, 128))
    row_ref[1] = jnp.broadcast_to(lax.rsqrt(var + 1e-06), (rows, 128))
    for copy in outs:
        copy.wait()
    for copy in sends + late:
        copy.wait_send()


def finish_kernel(hidden_hbm, row_hbm, mod_hbm, hidden_out, mlp_out, hbuf, mbuf, row, mod, sem, in_sem, out_sem, mlp_sem):
    rows, owned = hbuf.shape
    step = rows // CHUNKS
    small = [pltpu.make_async_copy(row_hbm, row, sem.at[0]), pltpu.make_async_copy(mod_hbm, mod, sem.at[1])]
    parts = [pl.ds(i * step, step) for i in range(CHUNKS)]
    loads = [pltpu.make_async_copy(hidden_hbm.at[at], hbuf.at[at], in_sem.at[i]) for i, at in enumerate(parts)]
    for copy in small + loads:
        copy.start()
    for copy in small:
        copy.wait()
    outs = []
    for i, at in enumerate(parts):
        loads[i].wait()
        outs.append(pltpu.make_async_copy(hbuf.at[at], hidden_out.at[at], out_sem.at[i]))
        outs[-1].start()
        for c in range(0, owned, 128):
            lane = slice(c, c + 128)
            wide = hbuf[at, lane].astype(jnp.float32)
            mbuf[at, lane] = (
                (wide - row[0, at]) * row[1, at] * (1.0 + mod[2:3, lane]) + mod[1:2, lane]
            ).astype(jnp.bfloat16)
        outs.append(pltpu.make_async_copy(mbuf.at[at], mlp_out.at[at], mlp_sem.at[i]))
        outs[-1].start()
    for copy in outs:
        copy.wait()


def fused_block(
    residual, query_proj, key_proj, value_proj, q_gain, k_gain, time_embed, time_proj, mod_table, out_weight
):
    rows, cols = query_proj.shape
    width = cols // LINE
    heads = width // HD
    owned = residual.shape[1]
    half_mod = mod_table.shape
    quarter = (half_mod[0], owned // PLANE)
    bf, f32 = jnp.bfloat16, jnp.float32
    dma = pltpu.SemaphoreType.DMA
    vmem = pl.BlockSpec(memory_space=pltpu.VMEM)
    hbm = pl.BlockSpec(memory_space=pl.ANY)
    blocks = LINE * PLANE
    count = heads * LINE * 2
    lines = time_proj.transpose(1, 0, 2)
    out = jax.ShapeDtypeStruct((rows, owned), bf)
    flat = pltpu.VMEM((rows, cols), bf)
    slab = pltpu.VMEM((heads, LINE, rows, HD), bf)
    lanes = pltpu.VMEM((2, rows, 128), f32)
    hidden, row, mod = pl.pallas_call(
        block_kernel,
        out_shape=(out, jax.ShapeDtypeStruct((2, rows, 128), f32), jax.ShapeDtypeStruct(half_mod, f32)),
        in_specs=[hbm, hbm, hbm, vmem, vmem, vmem, vmem, hbm, hbm, hbm],
        out_specs=(hbm, vmem, hbm),
        scratch_shapes=[
            flat, flat, flat, flat,
            pltpu.VMEM((heads, blocks, rows, HD), bf),
            pltpu.VMEM((heads, blocks, rows, HD), bf),
            slab, slab, slab,
            pltpu.VMEM((heads, LINE, rows, HD), f32),
            pltpu.VMEM((heads, LINE, rows, 2 * HD), f32),
            lanes, lanes, lanes,
            pltpu.VMEM((2,) + half_mod, f32),
            pltpu.VMEM(half_mod, f32),
            pltpu.VMEM(half_mod, f32),
            pltpu.VMEM((PLANE,) + quarter, f32),
            pltpu.VMEM((LINE + 1,) + quarter, f32),
            pltpu.VMEM(half_mod, f32),
            pltpu.VMEM(lines.shape, bf),
            pltpu.VMEM((heads, LINE * HD, owned), bf),
            pltpu.VMEM((heads, LINE * HD, owned), bf),
            slab,
            pltpu.VMEM((rows, owned), bf),
            pltpu.VMEM((rows, owned), f32),
            pltpu.VMEM((rows, owned), bf),
            lanes, lanes,
            dma((owned // TILE + 1,)),
            dma((3 * heads + 1,)), dma((4 + heads * LINE,)), dma((9 * heads,)), dma((9 * heads,)),
        ]
        + [dma((count,))] * 8
        + [dma((3 * heads,))] * 2
        + [dma((10,))] * 2
        + [dma((heads * LINE,))] * 2
        + [dma((heads,))] * 2
        + [dma((2,))] * 2,
        compiler_params=pltpu.CompilerParams(
            collective_id=0, has_side_effects=True, vmem_limit_bytes=60 * 1024 * 1024
        ),
    )(
        query_proj, key_proj, value_proj, q_gain, k_gain,
        time_embed.reshape(1, -1), mod_table, residual, lines, out_weight,
    )
    return pl.pallas_call(
        finish_kernel,
        out_shape=(out, out),
        in_specs=[hbm, hbm, hbm],
        out_specs=(hbm, hbm),
        scratch_shapes=[
            pltpu.VMEM((rows, owned), bf),
            pltpu.VMEM((rows, owned), bf),
            pltpu.VMEM((2, rows, 128), f32),
            pltpu.VMEM(half_mod, f32),
            dma((2,)), dma((CHUNKS,)), dma((CHUNKS,)), dma((CHUNKS,)),
        ],
        compiler_params=pltpu.CompilerParams(vmem_limit_bytes=60 * 1024 * 1024),
    )(hidden, row, mod)


def accumulate(carry, queries, keys_block, values_block):
    count = keys_block.shape[0]
    heads_here = queries.shape[1]
    keys_three = keys_block.reshape(count, heads_here, HD)
    values_three = values_block.reshape(count, heads_here, HD).astype(jnp.float32)
    scores = jnp.einsum("thd,shd->ths", queries, keys_three, preferred_element_type=jnp.float32) * (
        1.0 / math.sqrt(HD)
    )
    top_old, total_old, summed = carry
    top_new = jnp.maximum(top_old, jnp.max(scores, axis=2))
    weights = jnp.exp(scores - top_new[:, :, None])
    total_new = jnp.sum(weights, axis=2)
    summed_new = jnp.einsum("ths,shd->thd", weights, values_three, precision=lax.Precision.HIGHEST)
    return (top_new, total_new, summed_new)


def shards(
    residual,
    query_proj,
    key_proj,
    value_proj,
    q_gain,
    k_gain,
    time_embed,
    time_proj,
    mod_table,
    out_weight,
):
    if (
        lax.axis_size("head") == 2
        and lax.axis_size("frame") == LINE * PLANE
        and query_proj.shape[1] % (LINE * HD) == 0
    ):
        return fused_block(
            residual, query_proj, key_proj, value_proj, q_gain, k_gain, time_embed, time_proj, mod_table, out_weight
        )
    emb = jax.nn.silu(time_embed)
    partial_mod = jnp.einsum(
        "r,rcd->cd", emb, time_proj.astype(jnp.float32), precision=lax.Precision.HIGHEST
    )
    width = mod_table.shape[1]
    summed_mod = lax.psum(partial_mod, ("frame", "head"))
    share = lax.dynamic_slice_in_dim(summed_mod, lax.axis_index("head") * width, width, 1)
    modulation = mod_table + share
    gate = modulation[0]
    shift = modulation[1]
    scale = modulation[2]
    tok_rows = query_proj.shape[0]
    heads_here = query_proj.shape[1] // HD
    query_wide = query_proj.astype(jnp.float32)
    key_wide = key_proj.astype(jnp.float32)
    total_q, total_k = lax.psum(
        (jnp.sum(query_wide * query_wide, axis=1), jnp.sum(key_wide * key_wide, axis=1)), "head"
    )
    query_rms = lax.rsqrt(total_q / (HEADS * HD) + 1e-06)
    key_rms = lax.rsqrt(total_k / (HEADS * HD) + 1e-06)
    queries = (
        (query_wide * query_rms[:, None] * q_gain)
        .astype(jnp.bfloat16)
        .reshape(tok_rows, heads_here, HD)
    )
    start_state = (
        jnp.full((tok_rows, heads_here), -1e30, jnp.float32),
        jnp.zeros((tok_rows, heads_here), jnp.float32),
        jnp.zeros((tok_rows, heads_here, HD), jnp.float32),
    )
    every_scale = lax.all_gather(key_rms, "frame", axis=0, tiled=True)
    keys_block = (
        lax.all_gather(key_proj, "frame", axis=0, tiled=True).astype(jnp.float32)
        * every_scale[:, None]
        * k_gain
    ).astype(jnp.bfloat16)
    top_final, total_final, summed_final = accumulate(
        start_state, queries, keys_block, lax.all_gather(value_proj, "frame", axis=0, tiled=True)
    )
    attn = (
        (summed_final / total_final[:, :, None])
        .astype(jnp.bfloat16)
        .reshape(tok_rows, heads_here * HD)
    )
    proj = (
        lax.psum_scatter(
            lax.dot_general(
                out_weight, attn, (((0,), (1,)), ((), ())), preferred_element_type=jnp.float32
            ).astype(jnp.bfloat16),
            "head",
            scatter_dimension=0,
            tiled=True,
        )
        .astype(jnp.float32)
        .T
    )
    hidden_out = (residual.astype(jnp.float32) + gate * proj).astype(jnp.bfloat16)
    hidden32 = lax.optimization_barrier(hidden_out).astype(jnp.float32)
    row_sum, row_squares = lax.psum(
        (jnp.sum(hidden32, axis=1), jnp.sum(hidden32 * hidden32, axis=1)), "head"
    )
    mean = row_sum[:, None] / D
    var = row_squares[:, None] / D - mean * mean
    mlp_input = ((hidden32 - mean) * lax.rsqrt(var + 1e-06) * (1.0 + scale) + shift).astype(
        jnp.bfloat16
    )
    return (hidden_out, mlp_input)


def solution(mesh):
    in_specs = (
        P("frame", "head"),
        P("frame", "head"),
        P("frame", "head"),
        P("frame", "head"),
        P("head"),
        P("head"),
        P(("frame", "head")),
        P(("frame", "head"), None, None),
        P(None, "head"),
        P("head", None),
    )
    out_specs = (P("frame", "head"), P("frame", "head"))
    return jax.shard_map(shards, mesh=mesh, in_specs=in_specs, out_specs=out_specs, check_vma=False)
```
